32 devices in a mesh: groups: 2 (over y), seq: 4 (over x, core), chan: 4 (over z).
Axes of the slice: x: 2, y: 2, z: 4, core: 2. Of those that a mesh axis runs over, the one named last changes fastest.
Arguments:
- gate_input: bfloat16 [1024, 4096], P(('groups', 'seq'), 'chan'), parts along dimension 0, may hold values from -6 to 6
- value_input: bfloat16 [1024, 4096], P(('groups', 'seq'), 'chan'), parts along dimension 0, may hold values from -6 to 6
- short_filter: float32 [4096, 128], P('chan'), may hold values from -0.5 to 0.5
- long_filter: bfloat16 [512, 4096], P('seq', 'chan'), may hold values from -0.375 to 0.375
- query_weight: bfloat16 [32, 128, 128], P('chan'), may hold values from -0.5 to 0.5
- key_matrix: bfloat16 [1024, 4096], P(('groups', 'seq'), 'chan'), parts along dimension 0, may hold values from -200 to 200
- value_matrix: bfloat16 [1024, 4096], P(('groups', 'seq'), 'chan'), parts along dimension 0, may hold values from -6 to 6
Outputs:
- attended: bfloat16 [1024, 4096], P(('groups', 'seq'), 'chan'), parts along dimension 0
The draws below stay inside these ranges and needn't reach their ends.
There are 2 independent parts, one for each index of `groups`. The reference program is written for one: setup_inputs(seed, part) draws one part's arguments, and reference() takes and returns one part's arrays. A program takes and returns all parts, laid end to end along the dimension named above; an argument that names none is the same for every part. Nothing has to cross between parts.
All inputs are finite; a program needn't handle non-finite values.
Results may differ from the reference program's by a relative error of at most 0.011.
Values may be sent and summed in bfloat16 or wider, within the bound.
A program may use at most 64 MiB of HBM per device.

```python
import math
import jax
import jax.numpy as jnp
from jax import lax

HEADS = 32
HEAD_DIM = 128
TAPS = 128
DW = 4096
L = 512


def draw_key_matrix(key, part):
    base = jax.random.normal(jax.random.fold_in(key, 11), (L, DW), jnp.float32)
    return jnp.clip(base, -200.0, 200.0).astype(jnp.bfloat16)


def levels(rng, shape, cuts, smallest, largest):
    factor_of, own = 1.0, jax.random.fold_in(rng, 6)
    for position, shards_of in cuts:
        draws = jnp.exp(jax.random.uniform(jax.random.fold_in(own, position), (shards_of,), jnp.float32, smallest / len(cuts), largest / len(cuts)))
        factor_of = factor_of * jnp.repeat(draws, shape[position] // shards_of).reshape([-1 if axis == position else 1 for axis in range(len(shape))])
    return factor_of


def normal_values(rng, extent, deviation, bound, cuts=(), held_as=jnp.bfloat16):
    array = jax.random.normal(rng, extent, jnp.float32) * deviation
    if len(cuts) > 0:
        array = levels(rng, extent, cuts, -0.22, 0.18) * array
    return jnp.clip(array, min=-bound, max=bound).astype(held_as)


def setup_inputs(seed: int = 0, part: int = 0) -> dict:
    seeds = jax.random.split(jax.random.key(seed), 8)
    part_splits = jax.random.split(jax.random.fold_in(seeds[7], part), 8)
    gate_input = normal_values(part_splits[0], (L, DW), 1.0, 6.0, ((0, 4), (1, 4)))
    value_input = normal_values(part_splits[1], (L, DW), 1.0, 6.0, ((0, 4), (1, 4)))
    short_filter = normal_values(seeds[2], (DW, TAPS), TAPS ** -0.5, 0.5, ((0, 4),), jnp.float32)
    long_filter = normal_values(seeds[3], (L, DW), (L // 2) ** -0.5, 0.375, ((0, 4), (1, 4)))
    query_weight = normal_values(seeds[4], (HEADS, HEAD_DIM, HEAD_DIM), HEAD_DIM ** -0.5, 0.5, ((0, 4),))
    key_matrix = draw_key_matrix(jax.random.fold_in(jax.random.fold_in(seeds[7], part), 71), part)
    value_matrix = normal_values(part_splits[6], (L, DW), 1.0, 6.0, ((0, 4), (1, 4)))
    return dict(gate_input=gate_input, value_input=value_input, short_filter=short_filter, long_filter=long_filter, query_weight=query_weight, key_matrix=key_matrix, value_matrix=value_matrix)


def reference(gate_input, value_input, short_filter, long_filter, query_weight, key_matrix, value_matrix):
    width_block = math.gcd(DW, 256)
    block_count = DW // width_block
    gate_blocks = gate_input.reshape(L, block_count, width_block).transpose(1, 0, 2)
    value_blocks = value_input.reshape(L, block_count, width_block).transpose(1, 0, 2)
    filter_blocks = short_filter.reshape(block_count, width_block, TAPS)
    long_blocks = long_filter.reshape(L, block_count, width_block).transpose(1, 0, 2)

    def one_block(quad):
        gate_part, value_part, taps_part, long_part = quad
        padded = jnp.pad(gate_part.astype(jnp.float32), ((TAPS - 1, 0), (0, 0)))
        kernel = taps_part.astype(jnp.float32)[:, ::-1].T[:, None, :]
        smoothed = lax.conv_general_dilated(padded[None], kernel, (1,), 'VALID', dimension_numbers=('NHC', 'HIO', 'NHC'), feature_group_count=width_block, precision=lax.Precision.HIGHEST)[0]
        mixed_input = (smoothed * value_part.astype(jnp.float32)).astype(jnp.bfloat16)
        spec = jnp.fft.rfft(mixed_input.astype(jnp.float32), n=2 * L, axis=0) * jnp.fft.rfft(long_part.astype(jnp.float32), n=2 * L, axis=0)
        return jnp.fft.irfft(spec, n=2 * L, axis=0)[:L].astype(jnp.bfloat16)
    conv_blocks = lax.map(one_block, (gate_blocks, value_blocks, filter_blocks, long_blocks))
    conv_out = conv_blocks.transpose(1, 0, 2).reshape(L, DW)
    conv_heads = conv_out.reshape(L, HEADS, HEAD_DIM).astype(jnp.float32)
    queries = jnp.einsum('thd,hde->the', conv_heads, query_weight.astype(jnp.float32)).astype(jnp.bfloat16)
    query_heads = queries.transpose(1, 0, 2)
    key_heads = key_matrix.reshape(L, HEADS, HEAD_DIM).transpose(1, 0, 2)
    value_heads = value_matrix.reshape(L, HEADS, HEAD_DIM).transpose(1, 0, 2)
    block_rows = math.gcd(L, 1024)

    def one_head(triple):
        head_query, head_key, head_value = triple

        def one_rows(block_pair):
            block_query, block_first = block_pair
            scores = jnp.dot(block_query, head_key.T, preferred_element_type=jnp.float32) / math.sqrt(HEAD_DIM)
            query_pos = block_first + lax.iota(jnp.int32, block_rows)
            key_pos = lax.iota(jnp.int32, L)
            allowed = key_pos[None, :] <= query_pos[:, None]
            row_peak = lax.optimization_barrier(jnp.max(jnp.where(allowed, scores, -1e+30), axis=1, keepdims=True))
            weights = jnp.where(allowed, jnp.exp(scores - row_peak), 0.0)
            weight_sum = lax.optimization_barrier(jnp.sum(weights, axis=1, keepdims=True))
            product = jnp.dot(weights.astype(jnp.bfloat16), head_value, preferred_element_type=jnp.float32)
            return (product / weight_sum).astype(jnp.bfloat16)
        block_firsts = lax.iota(jnp.int32, L // block_rows) * block_rows
        blocks = head_query.reshape(L // block_rows, block_rows, HEAD_DIM)
        return lax.map(one_rows, (blocks, block_firsts)).reshape(L, HEAD_DIM)
    result = lax.map(one_head, (query_heads, key_heads, value_heads))
    return result.transpose(1, 0, 2).reshape(L, DW)
```

```python
import functools
import math

import jax
import jax.numpy as jnp
import numpy as np
from jax import lax
from jax.experimental import pallas as pl
from jax.experimental.pallas import tpu as pltpu
from jax.sharding import PartitionSpec as P

HEAD_DIM = 128
TAPS = 128
RADIX = 128


HIGHEST = lax.Precision.HIGHEST


def shifted(value, axis, steps):
    count = lax.axis_size(axis)
    initial, last = (max(0, -steps), min(count, count - steps))
    return lax.ppermute(value, axis, [(source, source + steps) for source in range(initial, last)])


def unit_table(height, breadth, modulus, orient):
    product = (
        lax.broadcasted_iota(jnp.int32, (height, breadth), 0)
        * lax.broadcasted_iota(jnp.int32, (height, breadth), 1)
        % modulus
    )
    angles = 2.0 * math.pi / modulus * product.astype(jnp.float32)
    return (jnp.cos(angles), orient * jnp.sin(angles))


def block_table(factor, orient):
    inner_re, inner_im = unit_table(factor, factor, factor, orient)
    upper = jnp.concatenate([inner_re, inner_im], axis=1)
    lower = jnp.concatenate([-inner_im, inner_re], axis=1)
    return jnp.concatenate([upper, lower], axis=0)


def spectrum(signal, factor):
    channels, length = signal.shape
    full_length = 2 * length
    column_count = full_length // factor
    folded = signal.reshape(channels, column_count // 2, factor)
    outer_re, outer_im = unit_table(column_count, column_count // 2, column_count, -1.0)
    outer_both = jnp.concatenate([outer_re, outer_im], axis=0)
    first = jnp.einsum("kn,cnm->ckm", outer_both, folded, precision=HIGHEST)
    first_re = first[:, :column_count]
    first_im = first[:, column_count:]
    twist_re, twist_im = unit_table(column_count, factor, full_length, -1.0)
    mid_re = first_re * twist_re - first_im * twist_im
    mid_im = first_re * twist_im + first_im * twist_re
    joined = jnp.concatenate([mid_re, mid_im], axis=2)
    return jnp.einsum("ckn,nm->ckm", joined, block_table(factor, -1.0), precision=HIGHEST)


def inverse(spec_both, factor, length):
    channels = spec_both.shape[0]
    full_length = 2 * length
    column_count = full_length // factor
    mid = jnp.einsum("ckm,mn->ckn", spec_both, block_table(factor, 1.0), precision=HIGHEST)
    mid_re = mid[:, :, :factor]
    mid_im = mid[:, :, factor:]
    twist_re, twist_im = unit_table(column_count, factor, full_length, 1.0)
    turn_re = mid_re * twist_re - mid_im * twist_im
    turn_im = mid_re * twist_im + mid_im * twist_re
    outer_re, outer_im = unit_table(column_count // 2, column_count, column_count, 1.0)
    outer_both = jnp.concatenate([outer_re, -outer_im], axis=1)
    turned = jnp.concatenate([turn_re, turn_im], axis=1)
    result = jnp.einsum("nk,ckm->cnm", outer_both, turned, precision=HIGHEST)
    return result.reshape(channels, length) / full_length


def general_shards(
    gate_input, value_input, short_filter, long_filter, query_weight, key_matrix, value_matrix
):
    seq_rows, local_width = gate_input.shape
    last_rows = gate_input[seq_rows - (TAPS - 1) :]
    earlier = shifted(last_rows, "seq", 1)
    padded = jnp.concatenate([earlier, gate_input], axis=0).astype(jnp.float32)
    kernel = short_filter[:, ::-1].T[:, None, :]
    smoothed = lax.conv_general_dilated(
        padded[None],
        kernel,
        (1,),
        "VALID",
        dimension_numbers=("NHC", "HIO", "NHC"),
        feature_group_count=local_width,
        precision=HIGHEST,
    )[0]
    mixed_input = (smoothed * value_input.astype(jnp.float32)).astype(jnp.bfloat16)
    signal, kernel_line = (
        lax.all_to_all(mixed_input.T, "seq", split_axis=0, concat_axis=1, tiled=True),
        lax.all_to_all(long_filter.T, "seq", split_axis=0, concat_axis=1, tiled=True),
    )
    length = signal.shape[1]
    signal_both = spectrum(signal.astype(jnp.float32), RADIX)
    kernel_both = spectrum(kernel_line.astype(jnp.float32), RADIX)
    signal_re = signal_both[:, :, :RADIX]
    signal_im = signal_both[:, :, RADIX:]
    kernel_re = kernel_both[:, :, :RADIX]
    kernel_im = kernel_both[:, :, RADIX:]
    joint = jnp.concatenate(
        [
            signal_re * kernel_re - signal_im * kernel_im,
            signal_re * kernel_im + signal_im * kernel_re,
        ],
        axis=2,
    )
    conv_line = inverse(joint, RADIX, length).astype(jnp.bfloat16)
    my_index = lax.axis_index("seq")
    group_firsts = [my_index * seq_rows]
    conv_columns = lax.all_to_all(conv_line, "seq", split_axis=1, concat_axis=0, tiled=True)
    heads_here = local_width // HEAD_DIM
    conv_heads = conv_columns.reshape(heads_here, HEAD_DIM, seq_rows)
    query_heads = jnp.einsum(
        "hds,hde->hse", conv_heads, query_weight, preferred_element_type=jnp.float32
    ).astype(jnp.bfloat16)
    group_count = len(group_firsts)
    query_groups = [query_heads]
    key_heads = key_matrix.reshape(seq_rows, heads_here, HEAD_DIM).transpose(1, 0, 2)
    value_heads = value_matrix.reshape(seq_rows, heads_here, HEAD_DIM).transpose(1, 0, 2)
    score_scale = 1.0 / math.sqrt(HEAD_DIM)

    def attend_group(running, group_query, group_first, key_block, value_block, first_row):
        block_rows = key_block.shape[1]

        def compute(current):
            peak_value, weight_sum, weighted = current
            scores = (
                jnp.einsum(
                    "hqd,hkd->hqk", group_query, key_block, preferred_element_type=jnp.float32
                )
                * score_scale
            )
            key_pos = first_row + lax.iota(jnp.int32, block_rows)
            query_pos = group_first + lax.iota(jnp.int32, seq_rows)
            allowed = (key_pos[None, :] <= query_pos[:, None])[None]
            scores = jnp.where(allowed, scores, -1e30)
            new_peak = jnp.maximum(peak_value, jnp.max(scores, axis=2))
            weights = jnp.where(allowed, jnp.exp(scores - new_peak[:, :, None]), 0.0)
            rescale = jnp.exp(peak_value - new_peak)
            weight_sum = weight_sum * rescale + jnp.sum(weights, axis=2)
            weighted = weighted * rescale[:, :, None] + jnp.einsum(
                "hqk,hkd->hqd",
                weights.astype(jnp.bfloat16),
                value_block,
                preferred_element_type=jnp.float32,
            )
            return (new_peak, weight_sum, weighted)

        live = first_row <= group_first + seq_rows - 1
        return lax.cond(live, compute, lambda current: current, running)

    def attend(states, key_block, value_block, first_row):
        return tuple(
            (
                attend_group(
                    states[g], query_groups[g], group_firsts[g], key_block, value_block, first_row
                )
                for g in range(group_count)
            )
        )

    one_state = (
        jnp.full((heads_here, seq_rows), -1e30, jnp.float32),
        jnp.zeros((heads_here, seq_rows), jnp.float32),
        jnp.zeros((heads_here, seq_rows, HEAD_DIM), jnp.float32),
    )
    initial = tuple((one_state for g in range(group_count)))
    running = initial
    key_piece = lax.all_gather(key_heads, "seq", axis=1, tiled=True)
    value_piece = lax.all_gather(value_heads, "seq", axis=1, tiled=True)
    piece_rows = key_piece.shape[1]
    block_rows = 512
    block_count = piece_rows // block_rows
    key_blocks = key_piece.reshape(heads_here, block_count, block_rows, HEAD_DIM).transpose(
        1, 0, 2, 3
    )
    value_blocks = value_piece.reshape(heads_here, block_count, block_rows, HEAD_DIM).transpose(
        1, 0, 2, 3
    )

    def advance(current, element):
        key_block, value_block, position = element
        return (attend(current, key_block, value_block, position * block_rows), None)

    running, _ = lax.scan(
        advance, running, (key_blocks, value_blocks, lax.iota(jnp.int32, block_count))
    )
    outputs = [state[2] / state[1][:, :, None] for state in running]
    result = outputs[0]
    attended_rows = result.transpose(1, 0, 2).reshape(seq_rows, local_width).astype(jnp.bfloat16)
    return attended_rows


def split_pair(array):
    high = array.astype(jnp.bfloat16)
    return high, (array - high.astype(jnp.float32)).astype(jnp.bfloat16)


def transform_tables(rows):
    full = 2 * rows
    turn = np.arange(rows)[:, None] * np.arange(full)[None, :] % full
    angle = 2.0 * np.pi / full * turn
    forward = np.concatenate([np.cos(angle), -np.sin(angle)], axis=0)
    forward[rows] = 1.0 - 2.0 * (np.arange(full) % 2)
    weight = np.full((full,), 2.0 / full)
    weight[0] = weight[rows] = 1.0 / full
    backward = (forward[:, :rows] * weight[:, None]).T
    return forward, backward


def host_split(table):
    high = table.astype(jnp.bfloat16)
    low = (table - high.astype(np.float64)).astype(jnp.bfloat16)
    return jnp.asarray(high), jnp.asarray(low)


def dot(a, b, contract=((1,), (0,))):
    return lax.dot_general(a, b, (contract, ((), ())), preferred_element_type=jnp.float32)


GATE, VALUE, LONG, KEY, VAL = range(5)
X_LONG, X_KEY, X_VAL = range(3)
(
    LOADS,
    WEIGHTS,
    OWN_GATE,
    OWN_VALUE,
    OWN_LONG,
    OWN_LATE,
    SENT,
    SENT_PAIR,
    SENT_OUT,
    HALO,
    PAIR_EARLY,
    PAIR_LONG,
    PAIR_LATE,
    PAIR_MIXED,
    FAR_GATE,
    FAR_VALUE,
    FAR_MIXED,
    FAR_LONG,
    PASSED,
    ARRIVED,
    FAR_HEADS,
) = [*range(18), 19, 20, 21]


def block_kernel(
    count,
    gate_in,
    value_in,
    long_in,
    key_in,
    val_in,
    short_in,
    weight_in,
    table_in,
    out,
    held,
    extra,
    table,
    short_taps,
    far_taps,
    far_gate,
    far_value,
    far_before,
    far_mixed,
    head_weight,
    grid_re,
    grid_im,
    grid_nyq,
    sig_re,
    sig_im,
    mixed,
    conv,
    weights,
    sums,
    result,
    sem,
):
    me = lax.axis_index("seq")
    my_group = lax.axis_index("groups")
    rows = gate_in.shape[0]
    width = held.shape[2]
    heads = width // HEAD_DIM
    half = count // 2
    low_rows = half * rows
    share = width // lax.axis_size("groups")
    streams = (gate_in, value_in, long_in, key_in, val_in)
    core = lax.rem(me, 2)
    late = me // 2
    is_low = late == 0
    is_high = late == 1
    partner = me + 1 - 2 * core
    opposite = lax.rem(me + half, count)
    far = [opposite, opposite + 1 - 2 * core]
    sibling = 1 - my_group
    fwd_high = table.at[: 2 * rows]
    fwd_low = table.at[2 * rows : 4 * rows]
    inv_high = table.at[4 * rows : 5 * rows]
    inv_low = table.at[5 * rows :]

    def span(index, size):
        return pl.ds(pl.multiple_of(index * size, size), size)

    def local(source, target, slot):
        return pltpu.make_async_copy(source, target, sem.at[slot])

    def remote(source, target, send, receive, **place):
        return pltpu.make_async_remote_copy(
            src_ref=source,
            dst_ref=target,
            send_sem=sem.at[send],
            recv_sem=sem.at[receive],
            device_id=place,
            device_id_type=pl.DeviceIdType.MESH,
        )

    def wait_for(view, slot):
        local(view, view, slot).wait()

    def wait_halves(halves, slot):
        wait_for(held.at[: count, : halves * rows // (2 * count)], slot)

    far_columns = span(1 - late, 2 * width)
    my_columns = span(me, width)
    other_columns = span(opposite, width)
    my_rows = span(me, rows)
    low_block = span(core, rows)
    for source, target, slot in (
        (table_in, table, LOADS),
        (short_in.at[far_columns], far_taps, LOADS),
        (gate_in.at[:, far_columns], far_gate, LOADS),
        (value_in.at[:, far_columns], far_value, LOADS),
        (short_in.at[my_columns], short_taps, LOADS),
        (gate_in.at[:, my_columns], held.at[GATE, my_rows], OWN_GATE),
        (value_in.at[:, my_columns], held.at[VALUE, my_rows], OWN_VALUE),
        (long_in.at[:, my_columns], held.at[LONG, my_rows], OWN_LONG),
        (long_in.at[:, other_columns], extra.at[X_LONG, low_block], OWN_LONG),
        (key_in.at[:, my_columns], held.at[KEY, my_rows], OWN_LATE),
        (val_in.at[:, my_columns], held.at[VAL, my_rows], OWN_LATE),
        (key_in.at[:, other_columns], extra.at[X_KEY, low_block], OWN_LATE),
        (val_in.at[:, other_columns], extra.at[X_VAL, low_block], OWN_LATE),
        (weight_in, head_weight, WEIGHTS),
    ):
        local(source, target, slot).start()

    barrier = pltpu.get_barrier_semaphore()
    for peer in (*far, partner):
        pl.semaphore_signal(
            barrier, inc=1, device_id={"seq": peer}, device_id_type=pl.DeviceIdType.MESH
        )
    pl.semaphore_signal(
        barrier, inc=1, device_id={"groups": sibling}, device_id_type=pl.DeviceIdType.MESH
    )
    pl.semaphore_wait(barrier, count)

    my_share = pl.ds(pl.multiple_of(my_group * share, share), share)

    def share_of(peer):
        return pl.ds(pl.multiple_of(peer * width + my_group * share, share), share)

    def to_partner(a, slot):
        return remote(
            streams[a].at[:, span(partner, width)],
            held.at[a, my_rows],
            SENT,
            slot,
            seq=partner,
        )

    def extra_to_partner(a, b, slot):
        return remote(
            streams[a].at[:, span(partner + half, width)],
            extra.at[b, low_block],
            SENT_PAIR,
            slot,
            seq=partner,
        )

    def raw_to(a, peer, slot):
        return remote(
            streams[a].at[:, span(peer, width)],
            held.at[a, my_rows],
            SENT_PAIR,
            slot,
            seq=peer,
        )

    def pass_on(parity):
        source = (1 - late) * half + parity
        piece = held.at[LONG, span(source, rows), my_share]
        return remote(piece, piece, SENT, PASSED, groups=sibling)

    @pl.when(core == 0)
    def _():
        remote(
            gate_in.at[:, far_columns], far_before, SENT_PAIR, HALO, seq=partner
        ).start()

    for peer in far:
        remote(
            long_in.at[:, share_of(peer)],
            held.at[LONG, my_rows, my_share],
            SENT,
            FAR_LONG + core,
            seq=peer,
        ).start()

    @pl.when(me == 1)
    def _():
        for peer in far:
            raw_to(GATE, peer, FAR_GATE).start()

    @pl.when(me == 2)
    def _():
        raw_to(GATE, opposite, FAR_GATE).start()
        for peer in far:
            raw_to(VALUE, peer, FAR_VALUE).start()

    to_partner(GATE, PAIR_EARLY).start()
    to_partner(VALUE, PAIR_EARLY).start()
    to_partner(LONG, PAIR_LONG).start()

    @pl.when(is_low)
    def _():
        extra_to_partner(LONG, X_LONG, PAIR_LONG).start()

    wait_halves(8 * count, LOADS)

    def forward(signal):
        depth = signal.shape[0]
        both = dot(fwd_high[:, :depth], signal) + dot(fwd_low[:, :depth], signal)
        return both[:rows], both[rows:]

    def backward(re, im):
        re_high, re_low = split_pair(re)
        im_high, im_low = split_pair(im)
        high = jnp.concatenate([re_high, im_high], axis=0)
        low = jnp.concatenate([re_low, im_low], axis=0)
        return dot(inv_high[...], high) + (dot(inv_low[...], high) + dot(inv_high[...], low))

    def factor_parts(re, im):
        first = lax.broadcasted_iota(jnp.int32, re.shape, 0) == 0
        return re, jnp.where(first, 0.0, im), jnp.where(first, im, re)

    last = ((1,), (1,))

    def taps_parts(taps):
        high, low = split_pair(taps[...])
        both = dot(fwd_high[:, :TAPS], high, last) + (
            dot(fwd_low[:, :TAPS], high, last) + dot(fwd_high[:, :TAPS], low, last)
        )
        return factor_parts(both[:rows], both[rows:])

    def smooth(signal, parts):
        re, im = forward(signal)
        re_part, im_part, nyq_part = parts
        return backward(re * re_part - im * im_part, re * im_part + im * nyq_part)

    @pl.when(me == 0)
    def _():
        far_before[...] = jnp.zeros_like(far_before)

    @pl.when(me != 2)
    def _():
        far_parts = taps_parts(far_taps)

        @pl.when(core == 1)
        def _():
            wait_for(far_before, HALO)

        @pl.when(me == 3)
        def _():
            remote(
                far_before.at[:, width:],
                held.at[GATE, half * rows : (half + 1) * rows],
                SENT_PAIR,
                FAR_GATE,
                seq=opposite,
            ).start()

        filtered = smooth(jnp.concatenate([far_gate[...], far_before[...]], axis=0), far_parts)
        far_mixed[...] = (filtered * far_value[...].astype(jnp.float32)).astype(jnp.bfloat16)
        for peer in far:
            remote(
                far_mixed.at[:, span(lax.rem(peer, 2), width)],
                mixed.at[my_rows],
                SENT,
                FAR_MIXED,
                seq=peer,
            ).start()

    extra_mixed = span(count + core, rows)

    @pl.when(is_low)
    def _():
        remote(
            far_mixed.at[:, span(1 - core, width)],
            mixed.at[extra_mixed],
            SENT_PAIR,
            PAIR_MIXED,
            seq=partner,
        ).start()
        local(far_mixed.at[:, span(core, width)], mixed.at[extra_mixed], PAIR_MIXED).start()

    for head in range(heads):
        for a in (KEY, VAL):
            for peer in far:
                remote(
                    streams[a].at[:, pl.ds(pl.multiple_of(peer * width + head * HEAD_DIM, HEAD_DIM), HEAD_DIM)],
                    held.at[a, my_rows, head * HEAD_DIM : (head + 1) * HEAD_DIM],
                    SENT,
                    FAR_HEADS + 3 * head + (0 if a == KEY else 1 + core),
                    seq=peer,
                ).start()
    to_partner(KEY, PAIR_LATE).start()
    to_partner(VAL, PAIR_LATE).start()

    @pl.when(is_low)
    def _():
        extra_to_partner(KEY, X_KEY, PAIR_LATE).start()
        extra_to_partner(VAL, X_VAL, PAIR_LATE).start()

    parts = taps_parts(short_taps)

    def rows_of(block):
        return slice(block * rows, (block + 1) * rows)

    def window(ref, block):
        now = ref[rows_of(block)]
        if block == 0:
            return now
        return jnp.concatenate([now, ref[rows_of(block - 1)]], axis=0)

    def mix(*blocks):
        for block in blocks:
            here = rows_of(block)
            filtered = smooth(window(held.at[GATE], block), parts)
            mixed[here] = (filtered * held[VALUE, here].astype(jnp.float32)).astype(jnp.bfloat16)

    def to_grid(ref, block, base=0):
        re, im, nyq = factor_parts(*forward(window(ref, block)))
        grid_re[base + block], grid_im[base + block], grid_nyq[base + block] = re, im, nyq

    def to_sig(*blocks):
        for block in blocks:
            sig_re[block], sig_im[block] = forward(mixed[rows_of(block)])

    def convolve(block, base=0):
        re = im = None
        for source in range(block + 1):
            at, lag = base + source, base + block - source
            s_re, s_im = sig_re[at], sig_im[at]
            re_term = s_re * grid_re[lag] - s_im * grid_im[lag]
            im_term = s_re * grid_im[lag] + s_im * grid_nyq[lag]
            re = re_term if re is None else re + re_term
            im = im_term if im is None else im + im_term
        conv[rows_of(base + block)] = backward(re, im).astype(jnp.bfloat16)

    def columns_of(head):
        return slice(head * HEAD_DIM, (head + 1) * HEAD_DIM)

    scale = 1.0 / math.sqrt(HEAD_DIM)

    def query(head, first, final, weight):
        here = slice(first * rows, final * rows)
        conv[here, columns_of(head)] = dot(conv[here, columns_of(head)], weight).astype(
            jnp.bfloat16
        )

    def score(head, block, keys, base=0):
        here = rows_of(base + block)
        past = (block + 1) * rows
        scores = dot(conv[here, columns_of(head)], keys[:past, columns_of(head)], last) * scale
        key_pos = lax.broadcasted_iota(jnp.int32, scores.shape, 1)
        query_pos = block * rows + lax.broadcasted_iota(jnp.int32, scores.shape, 0)
        allowed = key_pos <= query_pos
        scores = jnp.where(allowed, scores, -1e30)
        peak = jnp.max(scores, axis=1, keepdims=True)
        kept = jnp.where(allowed, jnp.exp(scores - peak), 0.0)
        sums[head, here] = jnp.broadcast_to(
            jnp.sum(kept, axis=1, keepdims=True), (rows, HEAD_DIM)
        )
        weights[head, here, :past] = kept.astype(jnp.bfloat16)

    def finish(head, block, values, base=0, owner=me):
        here = rows_of(base + block)
        past = (block + 1) * rows
        product = dot(weights[head, here, :past], values[:past, columns_of(head)])
        result[head, here] = (product / sums[head, here]).astype(jnp.bfloat16)
        source = result.at[head, here]
        target = out.at[:, pl.ds(pl.multiple_of(owner * width + head * HEAD_DIM, HEAD_DIM), HEAD_DIM)]

        @pl.when(me != block)
        def _():
            remote(source, target, SENT_OUT, ARRIVED, seq=block).start()

        @pl.when(me == block)
        def _():
            local(source, target, ARRIVED).start()

    wait_for(held.at[GATE, my_rows], OWN_GATE)
    wait_for(held.at[VALUE, my_rows], OWN_VALUE)
    wait_for(held.at[GATE, :low_rows], PAIR_EARLY)
    wait_for(held.at[LONG, :low_rows], OWN_LONG)

    @pl.when(is_low)
    def _():
        mix(0, 1)
        wait_for(held.at[LONG, :low_rows], PAIR_LONG)
        for block in range(half):
            to_grid(held.at[LONG], block)
            to_grid(extra.at[X_LONG], block, count)

    @pl.when(is_high)
    def _():
        mix(3)
        wait_for(held.at[LONG, :rows], PAIR_LONG)
        to_grid(held.at[LONG], 3)

    for parity in range(2):
        wait_for(held.at[LONG, :rows, :share], FAR_LONG + parity)
        pass_on(parity).start()

    @pl.when(is_low)
    def _():
        to_sig(0, 1)
        convolve(0)
        convolve(1)
        wait_for(held.at[LONG, :low_rows], PAIR_MIXED)
        to_sig(count, count + 1)
        convolve(0, count)
        convolve(1, count)
        wait_for(head_weight, WEIGHTS)
        wait_for(held.at[KEY], OWN_LATE)
        wait_for(held.at[KEY], PAIR_LATE)
        for head in range(heads):
            query(head, 0, half, head_weight[me * heads + head])
            query(head, count, count + half, head_weight[opposite * heads + head])
        for head in range(heads):
            for block in range(half):
                score(head, block, held.at[KEY])
                score(head, block, extra.at[X_KEY], count)
        for head in range(heads):
            for block in range(half):
                finish(head, block, held.at[VAL])
                finish(head, block, extra.at[X_VAL], count, opposite)

    @pl.when(is_high)
    def _():
        wait_for(head_weight, WEIGHTS)
        wait_for(held.at[KEY], OWN_LATE)
        wait_for(held.at[KEY, :low_rows], PAIR_LATE)

    wait_for(held.at[GATE, :rows], FAR_GATE)

    @pl.when(is_low)
    def _():
        wait_for(held.at[VALUE, :rows], FAR_VALUE)

    mix(2)
    wait_for(held.at[LONG, :low_rows, :share], PASSED)

    @pl.when(is_low)
    def _():
        to_grid(held.at[LONG], 3)

    @pl.when(is_high)
    def _():
        for block in range(half):
            to_grid(held.at[LONG], block)
        to_sig(3)

    to_grid(held.at[LONG], 2)
    to_sig(2)

    @pl.when(is_low)
    def _():
        wait_for(mixed.at[:rows], FAR_MIXED)
        to_sig(3)

    @pl.when(is_high)
    def _():
        wait_for(mixed.at[:low_rows], FAR_MIXED)
        to_sig(0, 1)

    convolve(2)
    convolve(3)
    for head in range(heads):
        query(head, half, count, head_weight[me * heads + head])
        first = FAR_HEADS + 3 * head
        wait_for(held.at[KEY, :low_rows, columns_of(head)], first)
        score(head, 2, held.at[KEY])
        score(head, 3, held.at[KEY])
        wait_for(held.at[VAL, :rows, columns_of(head)], first + 1)

        @pl.when(is_high)
        def _():
            wait_for(held.at[VAL, :rows, columns_of(head)], first + 2)

        finish(head, 2, held.at[VAL])

        @pl.when(is_low)
        def _():
            wait_for(held.at[VAL, :rows, columns_of(head)], first + 2)

        finish(head, 3, held.at[VAL])

    @pl.when(me == 2)
    def _():
        wait_halves(22, SENT)
        wait_halves(10, SENT_PAIR)

    @pl.when(me != 2)
    def _():
        wait_halves(26, SENT)

    @pl.when(me == 3)
    def _():
        wait_halves(2, SENT_PAIR)

    @pl.when(is_low)
    def _():
        wait_halves(12, SENT_PAIR)
        wait_halves(8, SENT_OUT)

    @pl.when(is_high)
    def _():
        wait_halves(2, SENT_OUT)

    wait_for(out, ARRIVED)


def head_shards(
    count,
    gate_input,
    value_input,
    short_filter,
    long_filter,
    query_weight,
    key_matrix,
    value_matrix,
):
    rows, local_width = gate_input.shape
    width = local_width // count
    heads = width // HEAD_DIM
    length = count * rows
    blocks = count + count // 2
    both_rows = blocks * rows
    forward, inverse_table = transform_tables(rows)
    table = jnp.concatenate([*host_split(forward), *host_split(inverse_table)], axis=0)
    bf16, f32 = jnp.bfloat16, jnp.float32
    return pl.pallas_call(
        functools.partial(block_kernel, count),
        out_shape=pltpu.VMEM((rows, local_width), bf16),
        in_specs=[pl.BlockSpec(memory_space=pl.ANY)] * 8,
        out_specs=pl.BlockSpec(memory_space=pltpu.VMEM),
        scratch_shapes=[
            pltpu.VMEM((5, length, width), bf16),
            pltpu.VMEM((3, length // 2, width), bf16),
            pltpu.VMEM((6 * rows, 2 * rows), bf16),
            pltpu.VMEM((width, TAPS), f32),
            pltpu.VMEM((2 * width, TAPS), f32),
            pltpu.VMEM((rows, 2 * width), bf16),
            pltpu.VMEM((rows, 2 * width), bf16),
            pltpu.VMEM((rows, 2 * width), bf16),
            pltpu.VMEM((rows, 2 * width), bf16),
            pltpu.VMEM(query_weight.shape, bf16),
            pltpu.VMEM((blocks, rows, width), f32),
            pltpu.VMEM((blocks, rows, width), f32),
            pltpu.VMEM((blocks, rows, width), f32),
            pltpu.VMEM((blocks, rows, width), f32),
            pltpu.VMEM((blocks, rows, width), f32),
            pltpu.VMEM((both_rows, width), bf16),
            pltpu.VMEM((both_rows, width), bf16),
            pltpu.VMEM((heads, both_rows, length), bf16),
            pltpu.VMEM((heads, both_rows, HEAD_DIM), f32),
            pltpu.VMEM((heads, both_rows, HEAD_DIM), bf16),
            pltpu.SemaphoreType.DMA((FAR_HEADS + 3 * heads,)),
        ],
        compiler_params=pltpu.CompilerParams(
            collective_id=0,
            has_side_effects=True,
        ),
    )(
        gate_input,
        value_input,
        long_filter,
        key_matrix,
        value_matrix,
        short_filter,
        query_weight,
        table,
    )


def shards(count, groups, gate_input, *others):
    rows, local_width = gate_input.shape
    by_heads = local_width % (count * groups * HEAD_DIM) == 0
    by_rows = rows >= TAPS and rows % HEAD_DIM == 0
    two_pairs = count == 4 and groups == 2
    if two_pairs and by_heads and by_rows:
        return head_shards(count, gate_input, *others)
    return general_shards(gate_input, *others)


def solution(mesh):
    in_specs = (
        P(("groups", "seq"), "chan"),
        P(("groups", "seq"), "chan"),
        P("chan", None),
        P("seq", "chan"),
        P("chan", None, None),
        P(("groups", "seq"), "chan"),
        P(("groups", "seq"), "chan"),
    )
    out_specs = P(("groups", "seq"), "chan")
    return jax.shard_map(
        functools.partial(shards, mesh.shape["seq"], mesh.shape["groups"]), mesh=mesh, in_specs=in_specs, out_specs=out_specs, check_vma=False)
```

```python
import functools
import math

import jax
import jax.numpy as jnp
import numpy as np
from jax import lax
from jax.experimental import pallas as pl
from jax.experimental.pallas import tpu as pltpu
from jax.sharding import PartitionSpec as P

HEAD_DIM = 128
TAPS = 128
RADIX = 128


HIGHEST = lax.Precision.HIGHEST


def shifted(value, axis, steps):
    count = lax.axis_size(axis)
    initial, last = (max(0, -steps), min(count, count - steps))
    return lax.ppermute(value, axis, [(source, source + steps) for source in range(initial, last)])


def unit_table(height, breadth, modulus, orient):
    product = (
        lax.broadcasted_iota(jnp.int32, (height, breadth), 0)
        * lax.broadcasted_iota(jnp.int32, (height, breadth), 1)
        % modulus
    )
    angles = 2.0 * math.pi / modulus * product.astype(jnp.float32)
    return (jnp.cos(angles), orient * jnp.sin(angles))


def block_table(factor, orient):
    inner_re, inner_im = unit_table(factor, factor, factor, orient)
    upper = jnp.concatenate([inner_re, inner_im], axis=1)
    lower = jnp.concatenate([-inner_im, inner_re], axis=1)
    return jnp.concatenate([upper, lower], axis=0)


def spectrum(signal, factor):
    channels, length = signal.shape
    full_length = 2 * length
    column_count = full_length // factor
    folded = signal.reshape(channels, column_count // 2, factor)
    outer_re, outer_im = unit_table(column_count, column_count // 2, column_count, -1.0)
    outer_both = jnp.concatenate([outer_re, outer_im], axis=0)
    first = jnp.einsum("kn,cnm->ckm", outer_both, folded, precision=HIGHEST)
    first_re = first[:, :column_count]
    first_im = first[:, column_count:]
    twist_re, twist_im = unit_table(column_count, factor, full_length, -1.0)
    mid_re = first_re * twist_re - first_im * twist_im
    mid_im = first_re * twist_im + first_im * twist_re
    joined = jnp.concatenate([mid_re, mid_im], axis=2)
    return jnp.einsum("ckn,nm->ckm", joined, block_table(factor, -1.0), precision=HIGHEST)


def inverse(spec_both, factor, length):
    channels = spec_both.shape[0]
    full_length = 2 * length
    column_count = full_length // factor
    mid = jnp.einsum("ckm,mn->ckn", spec_both, block_table(factor, 1.0), precision=HIGHEST)
    mid_re = mid[:, :, :factor]
    mid_im = mid[:, :, factor:]
    twist_re, twist_im = unit_table(column_count, factor, full_length, 1.0)
    turn_re = mid_re * twist_re - mid_im * twist_im
    turn_im = mid_re * twist_im + mid_im * twist_re
    outer_re, outer_im = unit_table(column_count // 2, column_count, column_count, 1.0)
    outer_both = jnp.concatenate([outer_re, -outer_im], axis=1)
    turned = jnp.concatenate([turn_re, turn_im], axis=1)
    result = jnp.einsum("nk,ckm->cnm", outer_both, turned, precision=HIGHEST)
    return result.reshape(channels, length) / full_length


def general_shards(
    gate_input, value_input, short_filter, long_filter, query_weight, key_matrix, value_matrix
):
    seq_rows, local_width = gate_input.shape
    last_rows = gate_input[seq_rows - (TAPS - 1) :]
    earlier = shifted(last_rows, "seq", 1)
    padded = jnp.concatenate([earlier, gate_input], axis=0).astype(jnp.float32)
    kernel = short_filter[:, ::-1].T[:, None, :]
    smoothed = lax.conv_general_dilated(
        padded[None],
        kernel,
        (1,),
        "VALID",
        dimension_numbers=("NHC", "HIO", "NHC"),
        feature_group_count=local_width,
        precision=HIGHEST,
    )[0]
    mixed_input = (smoothed * value_input.astype(jnp.float32)).astype(jnp.bfloat16)
    signal, kernel_line = (
        lax.all_to_all(mixed_input.T, "seq", split_axis=0, concat_axis=1, tiled=True),
        lax.all_to_all(long_filter.T, "seq", split_axis=0, concat_axis=1, tiled=True),
    )
    length = signal.shape[1]
    signal_both = spectrum(signal.astype(jnp.float32), RADIX)
    kernel_both = spectrum(kernel_line.astype(jnp.float32), RADIX)
    signal_re = signal_both[:, :, :RADIX]
    signal_im = signal_both[:, :, RADIX:]
    kernel_re = kernel_both[:, :, :RADIX]
    kernel_im = kernel_both[:, :, RADIX:]
    joint = jnp.concatenate(
        [
            signal_re * kernel_re - signal_im * kernel_im,
            signal_re * kernel_im + signal_im * kernel_re,
        ],
        axis=2,
    )
    conv_line = inverse(joint, RADIX, length).astype(jnp.bfloat16)
    my_index = lax.axis_index("seq")
    group_firsts = [my_index * seq_rows]
    conv_columns = lax.all_to_all(conv_line, "seq", split_axis=1, concat_axis=0, tiled=True)
    heads_here = local_width // HEAD_DIM
    conv_heads = conv_columns.reshape(heads_here, HEAD_DIM, seq_rows)
    query_heads = jnp.einsum(
        "hds,hde->hse", conv_heads, query_weight, preferred_element_type=jnp.float32
    ).astype(jnp.bfloat16)
    group_count = len(group_firsts)
    query_groups = [query_heads]
    key_heads = key_matrix.reshape(seq_rows, heads_here, HEAD_DIM).transpose(1, 0, 2)
    value_heads = value_matrix.reshape(seq_rows, heads_here, HEAD_DIM).transpose(1, 0, 2)
    score_scale = 1.0 / math.sqrt(HEAD_DIM)

    def attend_group(running, group_query, group_first, key_block, value_block, first_row):
        block_rows = key_block.shape[1]

        def compute(current):
            peak_value, weight_sum, weighted = current
            scores = (
                jnp.einsum(
                    "hqd,hkd->hqk", group_query, key_block, preferred_element_type=jnp.float32
                )
                * score_scale
            )
            key_pos = first_row + lax.iota(jnp.int32, block_rows)
            query_pos = group_first + lax.iota(jnp.int32, seq_rows)
            allowed = (key_pos[None, :] <= query_pos[:, None])[None]
            scores = jnp.where(allowed, scores, -1e30)
            new_peak = jnp.maximum(peak_value, jnp.max(scores, axis=2))
            weights = jnp.where(allowed, jnp.exp(scores - new_peak[:, :, None]), 0.0)
            rescale = jnp.exp(peak_value - new_peak)
            weight_sum = weight_sum * rescale + jnp.sum(weights, axis=2)
            weighted = weighted * rescale[:, :, None] + jnp.einsum(
                "hqk,hkd->hqd",
                weights.astype(jnp.bfloat16),
                value_block,
                preferred_element_type=jnp.float32,
            )
            return (new_peak, weight_sum, weighted)

        live = first_row <= group_first + seq_rows - 1
        return lax.cond(live, compute, lambda current: current, running)

    def attend(states, key_block, value_block, first_row):
        return tuple(
            (
                attend_group(
                    states[g], query_groups[g], group_firsts[g], key_block, value_block, first_row
                )
                for g in range(group_count)
            )
        )

    one_state = (
        jnp.full((heads_here, seq_rows), -1e30, jnp.float32),
        jnp.zeros((heads_here, seq_rows), jnp.float32),
        jnp.zeros((heads_here, seq_rows, HEAD_DIM), jnp.float32),
    )
    initial = tuple((one_state for g in range(group_count)))
    running = initial
    key_piece = lax.all_gather(key_heads, "seq", axis=1, tiled=True)
    value_piece = lax.all_gather(value_heads, "seq", axis=1, tiled=True)
    piece_rows = key_piece.shape[1]
    block_rows = 512
    block_count = piece_rows // block_rows
    key_blocks = key_piece.reshape(heads_here, block_count, block_rows, HEAD_DIM).transpose(
        1, 0, 2, 3
    )
    value_blocks = value_piece.reshape(heads_here, block_count, block_rows, HEAD_DIM).transpose(
        1, 0, 2, 3
    )

    def advance(current, element):
        key_block, value_block, position = element
        return (attend(current, key_block, value_block, position * block_rows), None)

    running, _ = lax.scan(
        advance, running, (key_blocks, value_blocks, lax.iota(jnp.int32, block_count))
    )
    outputs = [state[2] / state[1][:, :, None] for state in running]
    result = outputs[0]
    attended_rows = result.transpose(1, 0, 2).reshape(seq_rows, local_width).astype(jnp.bfloat16)
    return attended_rows


def split_pair(array):
    high = array.astype(jnp.bfloat16)
    return high, (array - high.astype(jnp.float32)).astype(jnp.bfloat16)


def transform_tables(rows):
    full = 2 * rows
    turn = np.arange(rows)[:, None] * np.arange(full)[None, :] % full
    angle = 2.0 * np.pi / full * turn
    forward = np.concatenate([np.cos(angle), -np.sin(angle)], axis=0)
    forward[rows] = 1.0 - 2.0 * (np.arange(full) % 2)
    weight = np.full((full,), 2.0 / full)
    weight[0] = weight[rows] = 1.0 / full
    backward = (forward[:, :rows] * weight[:, None]).T
    return forward, backward


def host_split(table):
    high = table.astype(jnp.bfloat16)
    low = (table - high.astype(np.float64)).astype(jnp.bfloat16)
    return jnp.asarray(high), jnp.asarray(low)


def dot(a, b, contract=((1,), (0,))):
    return lax.dot_general(a, b, (contract, ((), ())), preferred_element_type=jnp.float32)


GATE, VALUE, LONG, KEY, VAL = range(5)
X_LONG, X_KEY, X_VAL = range(3)
(
    LOADS,
    WEIGHTS,
    OWN_GATE,
    OWN_VALUE,
    OWN_LONG,
    OWN_LATE,
    SENT,
    SENT_PAIR,
    SENT_OUT,
    HALO,
    PAIR_EARLY,
    PAIR_LONG,
    PAIR_LATE,
    PAIR_MIXED,
    FAR_GATE,
    FAR_VALUE,
    FAR_MIXED,
    FAR_LONG,
    PASSED,
    ARRIVED,
    FAR_HEADS,
) = [*range(18), 19, 20, 21]


def block_kernel(
    count,
    gate_in,
    value_in,
    long_in,
    key_in,
    val_in,
    short_in,
    weight_in,
    table_in,
    out,
    held,
    extra,
    table,
    short_taps,
    far_taps,
    far_gate,
    far_value,
    far_before,
    far_mixed,
    head_weight,
    grid_re,
    grid_im,
    grid_nyq,
    sig_re,
    sig_im,
    mixed,
    conv,
    weights,
    sums,
    result,
    sem,
):
    me = lax.axis_index("seq")
    my_group = lax.axis_index("groups")
    rows = gate_in.shape[0]
    width = held.shape[2]
    heads = width // HEAD_DIM
    half = count // 2
    low_rows = half * rows
    share = width // lax.axis_size("groups")
    streams = (gate_in, value_in, long_in, key_in, val_in)
    core = lax.rem(me, 2)
    late = me // 2
    is_low = late == 0
    is_high = late == 1
    partner = me + 1 - 2 * core
    opposite = lax.rem(me + half, count)
    far = [opposite, opposite + 1 - 2 * core]
    sibling = 1 - my_group
    fwd_high = table.at[: 2 * rows]
    fwd_low = table.at[2 * rows : 4 * rows]
    inv_high = table.at[4 * rows : 5 * rows]
    inv_low = table.at[5 * rows :]

    def span(index, size):
        return pl.ds(pl.multiple_of(index * size, size), size)

    def local(source, target, slot):
        return pltpu.make_async_copy(source, target, sem.at[slot])

    def remote(source, target, send, receive, **place):
        return pltpu.make_async_remote_copy(
            src_ref=source,
            dst_ref=target,
            send_sem=sem.at[send],
            recv_sem=sem.at[receive],
            device_id=place,
            device_id_type=pl.DeviceIdType.MESH,
        )

    def wait_for(view, slot):
        local(view, view, slot).wait()

    def wait_halves(halves, slot):
        wait_for(held.at[: count, : halves * rows // (2 * count)], slot)

    far_columns = span(1 - late, 2 * width)
    my_columns = span(me, width)
    other_columns = span(opposite, width)
    my_rows = span(me, rows)
    low_block = span(core, rows)
    for source, target, slot in (
        (table_in, table, LOADS),
        (short_in.at[far_columns], far_taps, LOADS),
        (gate_in.at[:, far_columns], far_gate, LOADS),
        (value_in.at[:, far_columns], far_value, LOADS),
        (short_in.at[my_columns], short_taps, LOADS),
        (gate_in.at[:, my_columns], held.at[GATE, my_rows], OWN_GATE),
        (value_in.at[:, my_columns], held.at[VALUE, my_rows], OWN_VALUE),
        (long_in.at[:, my_columns], held.at[LONG, my_rows], OWN_LONG),
        (long_in.at[:, other_columns], extra.at[X_LONG, low_block], OWN_LONG),
        (key_in.at[:, my_columns], held.at[KEY, my_rows], OWN_LATE),
        (val_in.at[:, my_columns], held.at[VAL, my_rows], OWN_LATE),
        (key_in.at[:, other_columns], extra.at[X_KEY, low_block], OWN_LATE),
        (val_in.at[:, other_columns], extra.at[X_VAL, low_block], OWN_LATE),
        (weight_in, head_weight, WEIGHTS),
    ):
        local(source, target, slot).start()

    barrier = pltpu.get_barrier_semaphore()
    for peer in (*far, partner):
        pl.semaphore_signal(
            barrier, inc=1, device_id={"seq": peer}, device_id_type=pl.DeviceIdType.MESH
        )
    pl.semaphore_signal(
        barrier, inc=1, device_id={"groups": sibling}, device_id_type=pl.DeviceIdType.MESH
    )
    pl.semaphore_wait(barrier, count)

    my_share = pl.ds(pl.multiple_of(my_group * share, share), share)

    def share_of(peer):
        return pl.ds(pl.multiple_of(peer * width + my_group * share, share), share)

    def to_partner(a, slot):
        return remote(
            streams[a].at[:, span(partner, width)],
            held.at[a, my_rows],
            SENT,
            slot,
            seq=partner,
        )

    def extra_to_partner(a, b, slot):
        return remote(
            streams[a].at[:, span(partner + half, width)],
            extra.at[b, low_block],
            SENT_PAIR,
            slot,
            seq=partner,
        )

    def raw_to(a, peer, slot):
        return remote(
            streams[a].at[:, span(peer, width)],
            held.at[a, my_rows],
            SENT_PAIR,
            slot,
            seq=peer,
        )

    def pass_on(parity):
        source = (1 - late) * half + parity
        piece = held.at[LONG, span(source, rows), my_share]
        return remote(piece, piece, SENT, PASSED, groups=sibling)

    @pl.when(core == 0)
    def _():
        remote(
            gate_in.at[:, far_columns], far_before, SENT_PAIR, HALO, seq=partner
        ).start()

    for peer in far:
        remote(
            long_in.at[:, share_of(peer)],
            held.at[LONG, my_rows, my_share],
            SENT,
            FAR_LONG + core,
            seq=peer,
        ).start()

    @pl.when(me == 1)
    def _():
        for peer in far:
            raw_to(GATE, peer, FAR_GATE).start()

    @pl.when(me == 2)
    def _():
        for peer in far:
            raw_to(VALUE, peer, FAR_VALUE).start()

    to_partner(GATE, PAIR_EARLY).start()
    to_partner(VALUE, PAIR_EARLY).start()
    to_partner(LONG, PAIR_LONG).start()

    @pl.when(is_low)
    def _():
        extra_to_partner(LONG, X_LONG, PAIR_LONG).start()

    wait_halves(8 * count, LOADS)

    def forward(signal):
        depth = signal.shape[0]
        both = dot(fwd_high[:, :depth], signal) + dot(fwd_low[:, :depth], signal)
        return both[:rows], both[rows:]

    def backward(re, im):
        re_high, re_low = split_pair(re)
        im_high, im_low = split_pair(im)
        high = jnp.concatenate([re_high, im_high], axis=0)
        low = jnp.concatenate([re_low, im_low], axis=0)
        return dot(inv_high[...], high) + (dot(inv_low[...], high) + dot(inv_high[...], low))

    def factor_parts(re, im):
        first = lax.broadcasted_iota(jnp.int32, re.shape, 0) == 0
        return re, jnp.where(first, 0.0, im), jnp.where(first, im, re)

    last = ((1,), (1,))

    def taps_parts(taps):
        high, low = split_pair(taps[...])
        both = dot(fwd_high[:, :TAPS], high, last) + (
            dot(fwd_low[:, :TAPS], high, last) + dot(fwd_high[:, :TAPS], low, last)
        )
        return factor_parts(both[:rows], both[rows:])

    def smooth(signal, parts):
        re, im = forward(signal)
        re_part, im_part, nyq_part = parts
        return backward(re * re_part - im * im_part, re * im_part + im * nyq_part)

    @pl.when(me == 0)
    def _():
        far_before[...] = jnp.zeros_like(far_before)

    @pl.when(me != 2)
    def _():
        far_parts = taps_parts(far_taps)

        @pl.when(core == 1)
        def _():
            wait_for(far_before, HALO)

        @pl.when(me == 3)
        def _():
            for peer in range(half):
                remote(
                    far_before.at[:, peer * width : (peer + 1) * width],
                    held.at[GATE, half * rows : (half + 1) * rows],
                    SENT_PAIR,
                    FAR_GATE,
                    seq=peer,
                ).start()

        filtered = smooth(jnp.concatenate([far_gate[...], far_before[...]], axis=0), far_parts)
        far_mixed[...] = (filtered * far_value[...].astype(jnp.float32)).astype(jnp.bfloat16)
        for peer in far:
            remote(
                far_mixed.at[:, span(lax.rem(peer, 2), width)],
                mixed.at[my_rows],
                SENT,
                FAR_MIXED,
                seq=peer,
            ).start()

    extra_mixed = span(count + core, rows)

    @pl.when(is_low)
    def _():
        remote(
            far_mixed.at[:, span(1 - core, width)],
            mixed.at[extra_mixed],
            SENT_PAIR,
            PAIR_MIXED,
            seq=partner,
        ).start()
        local(far_mixed.at[:, span(core, width)], mixed.at[extra_mixed], PAIR_MIXED).start()

    first_far = (1 - late) * half
    for head in range(heads):
        for a in (KEY, VAL):
            for peer in (first_far, first_far + 1):
                remote(
                    streams[a].at[:, pl.ds(pl.multiple_of(peer * width + head * HEAD_DIM, HEAD_DIM), HEAD_DIM)],
                    held.at[a, my_rows, head * HEAD_DIM : (head + 1) * HEAD_DIM],
                    SENT,
                    FAR_HEADS + 3 * head + (0 if a == KEY else 1 + core),
                    seq=peer,
                ).start()
    to_partner(KEY, PAIR_LATE).start()
    to_partner(VAL, PAIR_LATE).start()

    @pl.when(is_low)
    def _():
        extra_to_partner(KEY, X_KEY, PAIR_LATE).start()
        extra_to_partner(VAL, X_VAL, PAIR_LATE).start()

    parts = taps_parts(short_taps)

    def rows_of(block):
        return slice(block * rows, (block + 1) * rows)

    def window(ref, block):
        now = ref[rows_of(block)]
        if block == 0:
            return now
        return jnp.concatenate([now, ref[rows_of(block - 1)]], axis=0)

    def mix(*blocks):
        for block in blocks:
            here = rows_of(block)
            filtered = smooth(window(held.at[GATE], block), parts)
            mixed[here] = (filtered * held[VALUE, here].astype(jnp.float32)).astype(jnp.bfloat16)

    def to_grid(ref, block, base=0):
        re, im, nyq = factor_parts(*forward(window(ref, block)))
        grid_re[base + block], grid_im[base + block], grid_nyq[base + block] = re, im, nyq

    def to_sig(*blocks):
        for block in blocks:
            sig_re[block], sig_im[block] = forward(mixed[rows_of(block)])

    def convolve(block, base=0):
        re = im = None
        for source in range(block + 1):
            at, lag = base + source, base + block - source
            s_re, s_im = sig_re[at], sig_im[at]
            re_term = s_re * grid_re[lag] - s_im * grid_im[lag]
            im_term = s_re * grid_im[lag] + s_im * grid_nyq[lag]
            re = re_term if re is None else re + re_term
            im = im_term if im is None else im + im_term
        conv[rows_of(base + block)] = backward(re, im).astype(jnp.bfloat16)

    def columns_of(head):
        return slice(head * HEAD_DIM, (head + 1) * HEAD_DIM)

    scale = 1.0 / math.sqrt(HEAD_DIM)

    def query(head, first, final, weight):
        here = slice(first * rows, final * rows)
        conv[here, columns_of(head)] = dot(conv[here, columns_of(head)], weight).astype(
            jnp.bfloat16
        )

    def score(head, block, keys, base=0):
        here = rows_of(base + block)
        past = (block + 1) * rows
        scores = dot(conv[here, columns_of(head)], keys[:past, columns_of(head)], last) * scale
        key_pos = lax.broadcasted_iota(jnp.int32, scores.shape, 1)
        query_pos = block * rows + lax.broadcasted_iota(jnp.int32, scores.shape, 0)
        allowed = key_pos <= query_pos
        scores = jnp.where(allowed, scores, -1e30)
        peak = jnp.max(scores, axis=1, keepdims=True)
        kept = jnp.where(allowed, jnp.exp(scores - peak), 0.0)
        sums[head, here] = jnp.broadcast_to(
            jnp.sum(kept, axis=1, keepdims=True), (rows, HEAD_DIM)
        )
        weights[head, here, :past] = kept.astype(jnp.bfloat16)

    def finish(head, block, values, base=0, owner=me):
        here = rows_of(base + block)
        past = (block + 1) * rows
        product = dot(weights[head, here, :past], values[:past, columns_of(head)])
        result[head, here] = (product / sums[head, here]).astype(jnp.bfloat16)
        source = result.at[head, here]
        target = out.at[:, pl.ds(pl.multiple_of(owner * width + head * HEAD_DIM, HEAD_DIM), HEAD_DIM)]

        @pl.when(me != block)
        def _():
            remote(source, target, SENT_OUT, ARRIVED, seq=block).start()

        @pl.when(me == block)
        def _():
            local(source, target, ARRIVED).start()

    wait_for(held.at[GATE, my_rows], OWN_GATE)
    wait_for(held.at[VALUE, my_rows], OWN_VALUE)
    wait_for(held.at[GATE, :low_rows], PAIR_EARLY)
    wait_for(held.at[LONG, :low_rows], OWN_LONG)

    @pl.when(is_low)
    def _():
        mix(0, 1)
        wait_for(held.at[LONG, :low_rows], PAIR_LONG)
        for block in range(half):
            to_grid(held.at[LONG], block)
            to_grid(extra.at[X_LONG], block, count)

    @pl.when(is_high)
    def _():
        mix(3)
        wait_for(held.at[LONG, :rows], PAIR_LONG)
        to_grid(held.at[LONG], 3)

    for parity in range(2):
        wait_for(held.at[LONG, :rows, :share], FAR_LONG + parity)
        pass_on(parity).start()

    @pl.when(is_low)
    def _():
        to_sig(0, 1)
        convolve(0)
        convolve(1)
        wait_for(held.at[LONG, :low_rows], PAIR_MIXED)
        to_sig(count, count + 1)
        convolve(0, count)
        convolve(1, count)
        wait_for(head_weight, WEIGHTS)
        wait_for(held.at[KEY], OWN_LATE)
        wait_for(held.at[KEY], PAIR_LATE)
        for head in range(heads):
            query(head, 0, half, head_weight[me * heads + head])
            query(head, count, count + half, head_weight[opposite * heads + head])
        for head in range(heads):
            for block in range(half):
                score(head, block, held.at[KEY])
                score(head, block, extra.at[X_KEY], count)
        for head in range(heads):
            for block in range(half):
                finish(head, block, held.at[VAL])
                finish(head, block, extra.at[X_VAL], count, opposite)

    @pl.when(is_high)
    def _():
        wait_for(head_weight, WEIGHTS)
        wait_for(held.at[KEY], OWN_LATE)
        wait_for(held.at[KEY, :low_rows], PAIR_LATE)

    wait_for(held.at[GATE, :rows], FAR_GATE)

    @pl.when(is_low)
    def _():
        wait_for(held.at[VALUE, :rows], FAR_VALUE)

    mix(2)
    wait_for(held.at[LONG, :low_rows, :share], PASSED)

    @pl.when(is_low)
    def _():
        to_grid(held.at[LONG], 3)

    @pl.when(is_high)
    def _():
        for block in range(half):
            to_grid(held.at[LONG], block)
        to_sig(3)

    to_grid(held.at[LONG], 2)
    to_sig(2)

    @pl.when(is_low)
    def _():
        wait_for(mixed.at[:rows], FAR_MIXED)
        to_sig(3)

    @pl.when(is_high)
    def _():
        wait_for(mixed.at[:low_rows], FAR_MIXED)
        to_sig(0, 1)

    convolve(2)
    convolve(3)
    for head in range(heads):
        query(head, half, count, head_weight[me * heads + head])
        first = FAR_HEADS + 3 * head
        wait_for(held.at[KEY, :low_rows, columns_of(head)], first)
        score(head, 2, held.at[KEY])
        score(head, 3, held.at[KEY])
        wait_for(held.at[VAL, :rows, columns_of(head)], first + 1)

        @pl.when(is_high)
        def _():
            wait_for(held.at[VAL, :rows, columns_of(head)], first + 2)

        finish(head, 2, held.at[VAL])

        @pl.when(is_low)
        def _():
            wait_for(held.at[VAL, :rows, columns_of(head)], first + 2)

        finish(head, 3, held.at[VAL])

    @pl.when(me == 2)
    def _():
        wait_halves(22, SENT)
        wait_halves(8, SENT_PAIR)

    @pl.when(me != 2)
    def _():
        wait_halves(26, SENT)

    @pl.when(me == 3)
    def _():
        wait_halves(4, SENT_PAIR)

    @pl.when(is_low)
    def _():
        wait_halves(12, SENT_PAIR)
        wait_halves(8, SENT_OUT)

    @pl.when(is_high)
    def _():
        wait_halves(2, SENT_OUT)

    wait_for(out, ARRIVED)


def head_shards(
    count,
    gate_input,
    value_input,
    short_filter,
    long_filter,
    query_weight,
    key_matrix,
    value_matrix,
):
    rows, local_width = gate_input.shape
    width = local_width // count
    heads = width // HEAD_DIM
    length = count * rows
    blocks = count + count // 2
    both_rows = blocks * rows
    forward, inverse_table = transform_tables(rows)
    table = jnp.concatenate([*host_split(forward), *host_split(inverse_table)], axis=0)
    bf16, f32 = jnp.bfloat16, jnp.float32
    return pl.pallas_call(
        functools.partial(block_kernel, count),
        out_shape=pltpu.VMEM((rows, local_width), bf16),
        in_specs=[pl.BlockSpec(memory_space=pl.ANY)] * 8,
        out_specs=pl.BlockSpec(memory_space=pltpu.VMEM),
        scratch_shapes=[
            pltpu.VMEM((5, length, width), bf16),
            pltpu.VMEM((3, length // 2, width), bf16),
            pltpu.VMEM((6 * rows, 2 * rows), bf16),
            pltpu.VMEM((width, TAPS), f32),
            pltpu.VMEM((2 * width, TAPS), f32),
            pltpu.VMEM((rows, 2 * width), bf16),
            pltpu.VMEM((rows, 2 * width), bf16),
            pltpu.VMEM((rows, 2 * width), bf16),
            pltpu.VMEM((rows, 2 * width), bf16),
            pltpu.VMEM(query_weight.shape, bf16),
            pltpu.VMEM((blocks, rows, width), f32),
            pltpu.VMEM((blocks, rows, width), f32),
            pltpu.VMEM((blocks, rows, width), f32),
            pltpu.VMEM((blocks, rows, width), f32),
            pltpu.VMEM((blocks, rows, width), f32),
            pltpu.VMEM((both_rows, width), bf16),
            pltpu.VMEM((both_rows, width), bf16),
            pltpu.VMEM((heads, both_rows, length), bf16),
            pltpu.VMEM((heads, both_rows, HEAD_DIM), f32),
            pltpu.VMEM((heads, both_rows, HEAD_DIM), bf16),
            pltpu.SemaphoreType.DMA((FAR_HEADS + 3 * heads,)),
        ],
        compiler_params=pltpu.CompilerParams(
            collective_id=0,
            has_side_effects=True,
        ),
    )(
        gate_input,
        value_input,
        long_filter,
        key_matrix,
        value_matrix,
        short_filter,
        query_weight,
        table,
    )


def shards(count, groups, gate_input, *others):
    rows, local_width = gate_input.shape
    by_heads = local_width % (count * groups * HEAD_DIM) == 0
    by_rows = rows >= TAPS and rows % HEAD_DIM == 0
    two_pairs = count == 4 and groups == 2
    if two_pairs and by_heads and by_rows:
        return head_shards(count, gate_input, *others)
    return general_shards(gate_input, *others)


def solution(mesh):
    in_specs = (
        P(("groups", "seq"), "chan"),
        P(("groups", "seq"), "chan"),
        P("chan", None),
        P("seq", "chan"),
        P("chan", None, None),
        P(("groups", "seq"), "chan"),
        P(("groups", "seq"), "chan"),
    )
    out_specs = P(("groups", "seq"), "chan")
    return jax.shard_map(
        functools.partial(shards, mesh.shape["seq"], mesh.shape["groups"]), mesh=mesh, in_specs=in_specs, out_specs=out_specs, check_vma=False)
```

```python
import functools
import math

import jax
import jax.numpy as jnp
import numpy as np
from jax import lax
from jax.experimental import pallas as pl
from jax.experimental.pallas import tpu as pltpu
from jax.sharding import PartitionSpec as P

HEAD_DIM = 128
TAPS = 128
RADIX = 128


HIGHEST = lax.Precision.HIGHEST


def shifted(value, axis, steps):
    count = lax.axis_size(axis)
    initial, last = (max(0, -steps), min(count, count - steps))
    return lax.ppermute(value, axis, [(source, source + steps) for source in range(initial, last)])


def unit_table(height, breadth, modulus, orient):
    product = (
        lax.broadcasted_iota(jnp.int32, (height, breadth), 0)
        * lax.broadcasted_iota(jnp.int32, (height, breadth), 1)
        % modulus
    )
    angles = 2.0 * math.pi / modulus * product.astype(jnp.float32)
    return (jnp.cos(angles), orient * jnp.sin(angles))


def block_table(factor, orient):
    inner_re, inner_im = unit_table(factor, factor, factor, orient)
    upper = jnp.concatenate([inner_re, inner_im], axis=1)
    lower = jnp.concatenate([-inner_im, inner_re], axis=1)
    return jnp.concatenate([upper, lower], axis=0)


def spectrum(signal, factor):
    channels, length = signal.shape
    full_length = 2 * length
    column_count = full_length // factor
    folded = signal.reshape(channels, column_count // 2, factor)
    outer_re, outer_im = unit_table(column_count, column_count // 2, column_count, -1.0)
    outer_both = jnp.concatenate([outer_re, outer_im], axis=0)
    first = jnp.einsum("kn,cnm->ckm", outer_both, folded, precision=HIGHEST)
    first_re = first[:, :column_count]
    first_im = first[:, column_count:]
    twist_re, twist_im = unit_table(column_count, factor, full_length, -1.0)
    mid_re = first_re * twist_re - first_im * twist_im
    mid_im = first_re * twist_im + first_im * twist_re
    joined = jnp.concatenate([mid_re, mid_im], axis=2)
    return jnp.einsum("ckn,nm->ckm", joined, block_table(factor, -1.0), precision=HIGHEST)


def inverse(spec_both, factor, length):
    channels = spec_both.shape[0]
    full_length = 2 * length
    column_count = full_length // factor
    mid = jnp.einsum("ckm,mn->ckn", spec_both, block_table(factor, 1.0), precision=HIGHEST)
    mid_re = mid[:, :, :factor]
    mid_im = mid[:, :, factor:]
    twist_re, twist_im = unit_table(column_count, factor, full_length, 1.0)
    turn_re = mid_re * twist_re - mid_im * twist_im
    turn_im = mid_re * twist_im + mid_im * twist_re
    outer_re, outer_im = unit_table(column_count // 2, column_count, column_count, 1.0)
    outer_both = jnp.concatenate([outer_re, -outer_im], axis=1)
    turned = jnp.concatenate([turn_re, turn_im], axis=1)
    result = jnp.einsum("nk,ckm->cnm", outer_both, turned, precision=HIGHEST)
    return result.reshape(channels, length) / full_length


def general_shards(
    gate_input, value_input, short_filter, long_filter, query_weight, key_matrix, value_matrix
):
    seq_rows, local_width = gate_input.shape
    last_rows = gate_input[seq_rows - (TAPS - 1) :]
    earlier = shifted(last_rows, "seq", 1)
    padded = jnp.concatenate([earlier, gate_input], axis=0).astype(jnp.float32)
    kernel = short_filter[:, ::-1].T[:, None, :]
    smoothed = lax.conv_general_dilated(
        padded[None],
        kernel,
        (1,),
        "VALID",
        dimension_numbers=("NHC", "HIO", "NHC"),
        feature_group_count=local_width,
        precision=HIGHEST,
    )[0]
    mixed_input = (smoothed * value_input.astype(jnp.float32)).astype(jnp.bfloat16)
    signal, kernel_line = (
        lax.all_to_all(mixed_input.T, "seq", split_axis=0, concat_axis=1, tiled=True),
        lax.all_to_all(long_filter.T, "seq", split_axis=0, concat_axis=1, tiled=True),
    )
    length = signal.shape[1]
    signal_both = spectrum(signal.astype(jnp.float32), RADIX)
    kernel_both = spectrum(kernel_line.astype(jnp.float32), RADIX)
    signal_re = signal_both[:, :, :RADIX]
    signal_im = signal_both[:, :, RADIX:]
    kernel_re = kernel_both[:, :, :RADIX]
    kernel_im = kernel_both[:, :, RADIX:]
    joint = jnp.concatenate(
        [
            signal_re * kernel_re - signal_im * kernel_im,
            signal_re * kernel_im + signal_im * kernel_re,
        ],
        axis=2,
    )
    conv_line = inverse(joint, RADIX, length).astype(jnp.bfloat16)
    my_index = lax.axis_index("seq")
    group_firsts = [my_index * seq_rows]
    conv_columns = lax.all_to_all(conv_line, "seq", split_axis=1, concat_axis=0, tiled=True)
    heads_here = local_width // HEAD_DIM
    conv_heads = conv_columns.reshape(heads_here, HEAD_DIM, seq_rows)
    query_heads = jnp.einsum(
        "hds,hde->hse", conv_heads, query_weight, preferred_element_type=jnp.float32
    ).astype(jnp.bfloat16)
    group_count = len(group_firsts)
    query_groups = [query_heads]
    key_heads = key_matrix.reshape(seq_rows, heads_here, HEAD_DIM).transpose(1, 0, 2)
    value_heads = value_matrix.reshape(seq_rows, heads_here, HEAD_DIM).transpose(1, 0, 2)
    score_scale = 1.0 / math.sqrt(HEAD_DIM)

    def attend_group(running, group_query, group_first, key_block, value_block, first_row):
        block_rows = key_block.shape[1]

        def compute(current):
            peak_value, weight_sum, weighted = current
            scores = (
                jnp.einsum(
                    "hqd,hkd->hqk", group_query, key_block, preferred_element_type=jnp.float32
                )
                * score_scale
            )
            key_pos = first_row + lax.iota(jnp.int32, block_rows)
            query_pos = group_first + lax.iota(jnp.int32, seq_rows)
            allowed = (key_pos[None, :] <= query_pos[:, None])[None]
            scores = jnp.where(allowed, scores, -1e30)
            new_peak = jnp.maximum(peak_value, jnp.max(scores, axis=2))
            weights = jnp.where(allowed, jnp.exp(scores - new_peak[:, :, None]), 0.0)
            rescale = jnp.exp(peak_value - new_peak)
            weight_sum = weight_sum * rescale + jnp.sum(weights, axis=2)
            weighted = weighted * rescale[:, :, None] + jnp.einsum(
                "hqk,hkd->hqd",
                weights.astype(jnp.bfloat16),
                value_block,
                preferred_element_type=jnp.float32,
            )
            return (new_peak, weight_sum, weighted)

        live = first_row <= group_first + seq_rows - 1
        return lax.cond(live, compute, lambda current: current, running)

    def attend(states, key_block, value_block, first_row):
        return tuple(
            (
                attend_group(
                    states[g], query_groups[g], group_firsts[g], key_block, value_block, first_row
                )
                for g in range(group_count)
            )
        )

    one_state = (
        jnp.full((heads_here, seq_rows), -1e30, jnp.float32),
        jnp.zeros((heads_here, seq_rows), jnp.float32),
        jnp.zeros((heads_here, seq_rows, HEAD_DIM), jnp.float32),
    )
    initial = tuple((one_state for g in range(group_count)))
    running = initial
    key_piece = lax.all_gather(key_heads, "seq", axis=1, tiled=True)
    value_piece = lax.all_gather(value_heads, "seq", axis=1, tiled=True)
    piece_rows = key_piece.shape[1]
    block_rows = 512
    block_count = piece_rows // block_rows
    key_blocks = key_piece.reshape(heads_here, block_count, block_rows, HEAD_DIM).transpose(
        1, 0, 2, 3
    )
    value_blocks = value_piece.reshape(heads_here, block_count, block_rows, HEAD_DIM).transpose(
        1, 0, 2, 3
    )

    def advance(current, element):
        key_block, value_block, position = element
        return (attend(current, key_block, value_block, position * block_rows), None)

    running, _ = lax.scan(
        advance, running, (key_blocks, value_blocks, lax.iota(jnp.int32, block_count))
    )
    outputs = [state[2] / state[1][:, :, None] for state in running]
    result = outputs[0]
    attended_rows = result.transpose(1, 0, 2).reshape(seq_rows, local_width).astype(jnp.bfloat16)
    return attended_rows


def split_pair(array):
    high = array.astype(jnp.bfloat16)
    return high, (array - high.astype(jnp.float32)).astype(jnp.bfloat16)


def transform_tables(rows):
    full = 2 * rows
    turn = np.arange(rows)[:, None] * np.arange(full)[None, :] % full
    angle = 2.0 * np.pi / full * turn
    forward = np.concatenate([np.cos(angle), -np.sin(angle)], axis=0)
    forward[rows] = 1.0 - 2.0 * (np.arange(full) % 2)
    weight = np.full((full,), 2.0 / full)
    weight[0] = weight[rows] = 1.0 / full
    backward = (forward[:, :rows] * weight[:, None]).T
    return forward, backward


def host_split(table):
    high = table.astype(jnp.bfloat16)
    low = (table - high.astype(np.float64)).astype(jnp.bfloat16)
    return jnp.asarray(high), jnp.asarray(low)


def dot(a, b, contract=((1,), (0,))):
    return lax.dot_general(a, b, (contract, ((), ())), preferred_element_type=jnp.float32)


GATE, VALUE, LONG, KEY, VAL = range(5)
X_LONG, X_KEY, X_VAL = range(3)
(
    LOADS,
    WEIGHTS,
    OWN_GATE,
    OWN_VALUE,
    OWN_LONG,
    OWN_LATE,
    SENT,
    SENT_PAIR,
    SENT_OUT,
    HALO,
    PAIR_EARLY,
    PAIR_LONG,
    PAIR_LATE,
    PAIR_MIXED,
    FAR_GATE,
    FAR_VALUE,
    FAR_MIXED,
    FAR_LONG,
    PASSED,
    ARRIVED,
    FAR_HEADS,
) = [*range(18), 19, 20, 21]


def block_kernel(
    count,
    gate_in,
    value_in,
    long_in,
    key_in,
    val_in,
    short_in,
    weight_in,
    table_in,
    out,
    held,
    extra,
    table,
    short_taps,
    far_taps,
    far_gate,
    far_value,
    far_before,
    far_mixed,
    head_weight,
    grid_re,
    grid_im,
    grid_nyq,
    sig_re,
    sig_im,
    mixed,
    conv,
    weights,
    sums,
    result,
    sem,
):
    me = lax.axis_index("seq")
    my_group = lax.axis_index("groups")
    rows = gate_in.shape[0]
    width = held.shape[2]
    heads = width // HEAD_DIM
    half = count // 2
    low_rows = half * rows
    share = width // lax.axis_size("groups")
    streams = (gate_in, value_in, long_in, key_in, val_in)
    core = lax.rem(me, 2)
    late = me // 2
    is_low = late == 0
    is_high = late == 1
    partner = me + 1 - 2 * core
    opposite = lax.rem(me + half, count)
    far = [opposite, opposite + 1 - 2 * core]
    sibling = 1 - my_group
    fwd_high = table.at[: 2 * rows]
    fwd_low = table.at[2 * rows : 4 * rows]
    inv_high = table.at[4 * rows : 5 * rows]
    inv_low = table.at[5 * rows :]

    def span(index, size):
        return pl.ds(pl.multiple_of(index * size, size), size)

    def local(source, target, slot):
        return pltpu.make_async_copy(source, target, sem.at[slot])

    def remote(source, target, send, receive, **place):
        return pltpu.make_async_remote_copy(
            src_ref=source,
            dst_ref=target,
            send_sem=sem.at[send],
            recv_sem=sem.at[receive],
            device_id=place,
            device_id_type=pl.DeviceIdType.MESH,
        )

    def wait_for(view, slot):
        local(view, view, slot).wait()

    def wait_halves(halves, slot):
        wait_for(held.at[: count, : halves * rows // (2 * count)], slot)

    far_columns = span(1 - late, 2 * width)
    my_columns = span(me, width)
    other_columns = span(opposite, width)
    my_rows = span(me, rows)
    low_block = span(core, rows)
    for source, target, slot in (
        (table_in, table, LOADS),
        (short_in.at[far_columns], far_taps, LOADS),
        (gate_in.at[:, far_columns], far_gate, LOADS),
        (value_in.at[:, far_columns], far_value, LOADS),
        (short_in.at[my_columns], short_taps, LOADS),
        (gate_in.at[:, my_columns], held.at[GATE, my_rows], OWN_GATE),
        (value_in.at[:, my_columns], held.at[VALUE, my_rows], OWN_VALUE),
        (long_in.at[:, my_columns], held.at[LONG, my_rows], OWN_LONG),
        (long_in.at[:, other_columns], extra.at[X_LONG, low_block], OWN_LONG),
        (key_in.at[:, my_columns], held.at[KEY, my_rows], OWN_LATE),
        (val_in.at[:, my_columns], held.at[VAL, my_rows], OWN_LATE),
        (key_in.at[:, other_columns], extra.at[X_KEY, low_block], OWN_LATE),
        (val_in.at[:, other_columns], extra.at[X_VAL, low_block], OWN_LATE),
        (weight_in, head_weight, WEIGHTS),
    ):
        local(source, target, slot).start()

    barrier = pltpu.get_barrier_semaphore()
    for peer in (*far, partner):
        pl.semaphore_signal(
            barrier, inc=1, device_id={"seq": peer}, device_id_type=pl.DeviceIdType.MESH
        )
    pl.semaphore_signal(
        barrier, inc=1, device_id={"groups": sibling}, device_id_type=pl.DeviceIdType.MESH
    )
    pl.semaphore_wait(barrier, count)

    my_share = pl.ds(pl.multiple_of(my_group * share, share), share)

    def share_of(peer):
        return pl.ds(pl.multiple_of(peer * width + my_group * share, share), share)

    def to_partner(a, slot):
        return remote(
            streams[a].at[:, span(partner, width)],
            held.at[a, my_rows],
            SENT,
            slot,
            seq=partner,
        )

    def extra_to_partner(a, b, slot):
        return remote(
            streams[a].at[:, span(partner + half, width)],
            extra.at[b, low_block],
            SENT_PAIR,
            slot,
            seq=partner,
        )

    def raw_to(a, peer, slot):
        return remote(
            streams[a].at[:, span(peer, width)],
            held.at[a, my_rows],
            SENT_PAIR,
            slot,
            seq=peer,
        )

    def pass_on(parity):
        source = (1 - late) * half + parity
        piece = held.at[LONG, span(source, rows), my_share]
        return remote(piece, piece, SENT, PASSED, groups=sibling)

    @pl.when(core == 0)
    def _():
        remote(
            gate_in.at[:, far_columns], far_before, SENT_PAIR, HALO, seq=partner
        ).start()

    @pl.when(me == 1)
    def _():
        remote(
            gate_in.at[:, my_columns],
            far_before.at[:, width:],
            SENT_PAIR,
            HALO,
            seq=far[1],
        ).start()

    for peer in far:
        remote(
            long_in.at[:, share_of(peer)],
            held.at[LONG, my_rows, my_share],
            SENT,
            FAR_LONG + core,
            seq=peer,
        ).start()

    @pl.when(me == 1)
    def _():
        for peer in far:
            raw_to(GATE, peer, FAR_GATE).start()

    @pl.when(me == 2)
    def _():
        raw_to(VALUE, opposite, FAR_VALUE).start()

    to_partner(GATE, PAIR_EARLY).start()
    to_partner(VALUE, PAIR_EARLY).start()
    to_partner(LONG, PAIR_LONG).start()

    @pl.when(is_low)
    def _():
        extra_to_partner(LONG, X_LONG, PAIR_LONG).start()

    wait_halves(8 * count, LOADS)

    def forward(signal):
        depth = signal.shape[0]
        both = dot(fwd_high[:, :depth], signal) + dot(fwd_low[:, :depth], signal)
        return both[:rows], both[rows:]

    def backward(re, im):
        re_high, re_low = split_pair(re)
        im_high, im_low = split_pair(im)
        high = jnp.concatenate([re_high, im_high], axis=0)
        low = jnp.concatenate([re_low, im_low], axis=0)
        return dot(inv_high[...], high) + (dot(inv_low[...], high) + dot(inv_high[...], low))

    def factor_parts(re, im):
        first = lax.broadcasted_iota(jnp.int32, re.shape, 0) == 0
        return re, jnp.where(first, 0.0, im), jnp.where(first, im, re)

    last = ((1,), (1,))

    def taps_parts(taps):
        high, low = split_pair(taps[...])
        both = dot(fwd_high[:, :TAPS], high, last) + (
            dot(fwd_low[:, :TAPS], high, last) + dot(fwd_high[:, :TAPS], low, last)
        )
        return factor_parts(both[:rows], both[rows:])

    def smooth(signal, parts):
        re, im = forward(signal)
        re_part, im_part, nyq_part = parts
        return backward(re * re_part - im * im_part, re * im_part + im * nyq_part)

    @pl.when(me == 0)
    def _():
        far_before[...] = jnp.zeros_like(far_before)

    @pl.when(me != 2)
    def _():
        far_parts = taps_parts(far_taps)

        @pl.when(core == 1)
        def _():
            wait_for(far_before, HALO)

        @pl.when(me == 3)
        def _():
            remote(
                far_before.at[:, :width],
                held.at[GATE, half * rows : (half + 1) * rows],
                SENT_PAIR,
                FAR_GATE,
                seq=0,
            ).start()

        filtered = smooth(jnp.concatenate([far_gate[...], far_before[...]], axis=0), far_parts)
        far_mixed[...] = (filtered * far_value[...].astype(jnp.float32)).astype(jnp.bfloat16)
        for peer in far:
            remote(
                far_mixed.at[:, span(lax.rem(peer, 2), width)],
                mixed.at[my_rows],
                SENT,
                FAR_MIXED,
                seq=peer,
            ).start()

    extra_mixed = span(count + core, rows)

    @pl.when(is_low)
    def _():
        remote(
            far_mixed.at[:, span(1 - core, width)],
            mixed.at[extra_mixed],
            SENT_PAIR,
            PAIR_MIXED,
            seq=partner,
        ).start()
        local(far_mixed.at[:, span(core, width)], mixed.at[extra_mixed], PAIR_MIXED).start()

    first_far = (1 - late) * half

    def send_heads(head, *arrays):
        here = head * HEAD_DIM
        for a in arrays:
            for peer in (first_far, first_far + 1):
                remote(
                    streams[a].at[:, pl.ds(pl.multiple_of(peer * width + here, HEAD_DIM), HEAD_DIM)],
                    held.at[a, my_rows, here : here + HEAD_DIM],
                    SENT,
                    FAR_HEADS + 3 * head + (0 if a == KEY else 1 + core),
                    seq=peer,
                ).start()

    send_heads(0, KEY)

    @pl.when(me == 2)
    def _():
        near_parts = taps_parts(far_taps.at[width:])
        wait_for(far_before.at[:, width:], HALO)
        filtered = smooth(
            jnp.concatenate([far_gate[:, width:], far_before[:, width:]], axis=0), near_parts
        )
        far_mixed[:, width:] = (filtered * far_value[:, width:].astype(jnp.float32)).astype(
            jnp.bfloat16
        )
        remote(
            far_mixed.at[:, width:], mixed.at[my_rows], SENT_PAIR, FAR_MIXED, seq=1
        ).start()

    send_heads(0, VAL)
    for head in range(1, heads):
        send_heads(head, KEY, VAL)
    to_partner(KEY, PAIR_LATE).start()
    to_partner(VAL, PAIR_LATE).start()

    @pl.when(is_low)
    def _():
        extra_to_partner(KEY, X_KEY, PAIR_LATE).start()
        extra_to_partner(VAL, X_VAL, PAIR_LATE).start()

    parts = taps_parts(short_taps)

    def rows_of(block):
        return slice(block * rows, (block + 1) * rows)

    def window(ref, block):
        now = ref[rows_of(block)]
        if block == 0:
            return now
        return jnp.concatenate([now, ref[rows_of(block - 1)]], axis=0)

    def mix(*blocks):
        for block in blocks:
            here = rows_of(block)
            filtered = smooth(window(held.at[GATE], block), parts)
            mixed[here] = (filtered * held[VALUE, here].astype(jnp.float32)).astype(jnp.bfloat16)

    def to_grid(ref, block, base=0):
        re, im, nyq = factor_parts(*forward(window(ref, block)))
        grid_re[base + block], grid_im[base + block], grid_nyq[base + block] = re, im, nyq

    def to_sig(*blocks):
        for block in blocks:
            sig_re[block], sig_im[block] = forward(mixed[rows_of(block)])

    def convolve(block, base=0):
        re = im = None
        for source in range(block + 1):
            at, lag = base + source, base + block - source
            s_re, s_im = sig_re[at], sig_im[at]
            re_term = s_re * grid_re[lag] - s_im * grid_im[lag]
            im_term = s_re * grid_im[lag] + s_im * grid_nyq[lag]
            re = re_term if re is None else re + re_term
            im = im_term if im is None else im + im_term
        conv[rows_of(base + block)] = backward(re, im).astype(jnp.bfloat16)

    def columns_of(head):
        return slice(head * HEAD_DIM, (head + 1) * HEAD_DIM)

    scale = 1.0 / math.sqrt(HEAD_DIM)

    def query(head, first, final, weight):
        here = slice(first * rows, final * rows)
        conv[here, columns_of(head)] = dot(conv[here, columns_of(head)], weight).astype(
            jnp.bfloat16
        )

    def score(head, block, keys, base=0):
        here = rows_of(base + block)
        past = (block + 1) * rows
        scores = dot(conv[here, columns_of(head)], keys[:past, columns_of(head)], last) * scale
        key_pos = lax.broadcasted_iota(jnp.int32, scores.shape, 1)
        query_pos = block * rows + lax.broadcasted_iota(jnp.int32, scores.shape, 0)
        allowed = key_pos <= query_pos
        scores = jnp.where(allowed, scores, -1e30)
        peak = jnp.max(scores, axis=1, keepdims=True)
        kept = jnp.where(allowed, jnp.exp(scores - peak), 0.0)
        sums[head, here] = jnp.broadcast_to(
            jnp.sum(kept, axis=1, keepdims=True), (rows, HEAD_DIM)
        )
        weights[head, here, :past] = kept.astype(jnp.bfloat16)

    def finish(head, block, values, base=0, owner=me):
        here = rows_of(base + block)
        past = (block + 1) * rows
        product = dot(weights[head, here, :past], values[:past, columns_of(head)])
        result[head, here] = (product / sums[head, here]).astype(jnp.bfloat16)
        source = result.at[head, here]
        target = out.at[:, pl.ds(pl.multiple_of(owner * width + head * HEAD_DIM, HEAD_DIM), HEAD_DIM)]

        @pl.when(me != block)
        def _():
            remote(source, target, SENT_OUT, ARRIVED, seq=block).start()

        @pl.when(me == block)
        def _():
            local(source, target, ARRIVED).start()

    wait_for(held.at[GATE, my_rows], OWN_GATE)
    wait_for(held.at[VALUE, my_rows], OWN_VALUE)
    wait_for(held.at[GATE, :low_rows], PAIR_EARLY)
    wait_for(held.at[LONG, :low_rows], OWN_LONG)

    @pl.when(is_low)
    def _():
        mix(0, 1)
        wait_for(held.at[LONG, :low_rows], PAIR_LONG)
        for block in range(half):
            to_grid(held.at[LONG], block)
            to_grid(extra.at[X_LONG], block, count)

    @pl.when(is_high)
    def _():
        mix(3)
        wait_for(held.at[LONG, :rows], PAIR_LONG)
        to_grid(held.at[LONG], 3)

    for parity in range(2):
        wait_for(held.at[LONG, :rows, :share], FAR_LONG + parity)
        pass_on(parity).start()

    @pl.when(is_low)
    def _():
        to_sig(0, 1)
        convolve(0)
        convolve(1)
        wait_for(held.at[LONG, :low_rows], PAIR_MIXED)
        to_sig(count, count + 1)
        convolve(0, count)
        convolve(1, count)
        wait_for(head_weight, WEIGHTS)
        wait_for(held.at[KEY], OWN_LATE)
        wait_for(held.at[KEY], PAIR_LATE)
        for head in range(heads):
            query(head, 0, half, head_weight[me * heads + head])
            query(head, count, count + half, head_weight[opposite * heads + head])
        for head in range(heads):
            for block in range(half):
                score(head, block, held.at[KEY])
                score(head, block, extra.at[X_KEY], count)
        for head in range(heads):
            for block in range(half):
                finish(head, block, held.at[VAL])
                finish(head, block, extra.at[X_VAL], count, opposite)

    @pl.when(is_high)
    def _():
        wait_for(head_weight, WEIGHTS)
        wait_for(held.at[KEY], OWN_LATE)
        wait_for(held.at[KEY, :low_rows], PAIR_LATE)

    @pl.when(me == 0)
    def _():
        wait_for(held.at[VALUE, :rows], FAR_VALUE)

    @pl.when(me != 1)
    def _():
        wait_for(held.at[GATE, :rows], FAR_GATE)
        mix(2)

    wait_for(held.at[LONG, :low_rows, :share], PASSED)

    @pl.when(is_low)
    def _():
        to_grid(held.at[LONG], 3)

    @pl.when(is_high)
    def _():
        for block in range(half):
            to_grid(held.at[LONG], block)
        to_sig(3)

    to_grid(held.at[LONG], 2)

    @pl.when(me == 0)
    def _():
        wait_for(mixed.at[:rows], FAR_MIXED)

    @pl.when(me != 0)
    def _():
        wait_for(mixed.at[:low_rows], FAR_MIXED)

    @pl.when(is_low)
    def _():
        to_sig(3)

    @pl.when(is_high)
    def _():
        to_sig(0, 1)

    to_sig(2)
    convolve(2)
    convolve(3)
    for head in range(heads):
        query(head, half, count, head_weight[me * heads + head])
        first = FAR_HEADS + 3 * head
        wait_for(held.at[KEY, :low_rows, columns_of(head)], first)
        score(head, 2, held.at[KEY])
        score(head, 3, held.at[KEY])
        wait_for(held.at[VAL, :rows, columns_of(head)], first + 1)

        @pl.when(is_high)
        def _():
            wait_for(held.at[VAL, :rows, columns_of(head)], first + 2)

        finish(head, 2, held.at[VAL])

        @pl.when(is_low)
        def _():
            wait_for(held.at[VAL, :rows, columns_of(head)], first + 2)

        finish(head, 3, held.at[VAL])

    @pl.when(me == 2)
    def _():
        wait_halves(22, SENT)
        wait_halves(8, SENT_PAIR)

    @pl.when(me != 2)
    def _():
        wait_halves(26, SENT)

    @pl.when(me == 3)
    def _():
        wait_halves(2, SENT_PAIR)

    @pl.when(me == 0)
    def _():
        wait_halves(12, SENT_PAIR)

    @pl.when(me == 1)
    def _():
        wait_halves(14, SENT_PAIR)

    @pl.when(is_low)
    def _():
        wait_halves(8, SENT_OUT)

    @pl.when(is_high)
    def _():
        wait_halves(2, SENT_OUT)

    wait_for(out, ARRIVED)


def head_shards(
    count,
    gate_input,
    value_input,
    short_filter,
    long_filter,
    query_weight,
    key_matrix,
    value_matrix,
):
    rows, local_width = gate_input.shape
    width = local_width // count
    heads = width // HEAD_DIM
    length = count * rows
    blocks = count + count // 2
    both_rows = blocks * rows
    forward, inverse_table = transform_tables(rows)
    table = jnp.concatenate([*host_split(forward), *host_split(inverse_table)], axis=0)
    bf16, f32 = jnp.bfloat16, jnp.float32
    return pl.pallas_call(
        functools.partial(block_kernel, count),
        out_shape=pltpu.VMEM((rows, local_width), bf16),
        in_specs=[pl.BlockSpec(memory_space=pl.ANY)] * 8,
        out_specs=pl.BlockSpec(memory_space=pltpu.VMEM),
        scratch_shapes=[
            pltpu.VMEM((5, length, width), bf16),
            pltpu.VMEM((3, length // 2, width), bf16),
            pltpu.VMEM((6 * rows, 2 * rows), bf16),
            pltpu.VMEM((width, TAPS), f32),
            pltpu.VMEM((2 * width, TAPS), f32),
            pltpu.VMEM((rows, 2 * width), bf16),
            pltpu.VMEM((rows, 2 * width), bf16),
            pltpu.VMEM((rows, 2 * width), bf16),
            pltpu.VMEM((rows, 2 * width), bf16),
            pltpu.VMEM(query_weight.shape, bf16),
            pltpu.VMEM((blocks, rows, width), f32),
            pltpu.VMEM((blocks, rows, width), f32),
            pltpu.VMEM((blocks, rows, width), f32),
            pltpu.VMEM((blocks, rows, width), f32),
            pltpu.VMEM((blocks, rows, width), f32),
            pltpu.VMEM((both_rows, width), bf16),
            pltpu.VMEM((both_rows, width), bf16),
            pltpu.VMEM((heads, both_rows, length), bf16),
            pltpu.VMEM((heads, both_rows, HEAD_DIM), f32),
            pltpu.VMEM((heads, both_rows, HEAD_DIM), bf16),
            pltpu.SemaphoreType.DMA((FAR_HEADS + 3 * heads,)),
        ],
        compiler_params=pltpu.CompilerParams(
            collective_id=0,
            has_side_effects=True,
        ),
    )(
        gate_input,
        value_input,
        long_filter,
        key_matrix,
        value_matrix,
        short_filter,
        query_weight,
        table,
    )


def shards(count, groups, gate_input, *others):
    rows, local_width = gate_input.shape
    by_heads = local_width % (count * groups * HEAD_DIM) == 0
    by_rows = rows >= TAPS and rows % HEAD_DIM == 0
    two_pairs = count == 4 and groups == 2
    if two_pairs and by_heads and by_rows:
        return head_shards(count, gate_input, *others)
    return general_shards(gate_input, *others)


def solution(mesh):
    in_specs = (
        P(("groups", "seq"), "chan"),
        P(("groups", "seq"), "chan"),
        P("chan", None),
        P("seq", "chan"),
        P("chan", None, None),
        P(("groups", "seq"), "chan"),
        P(("groups", "seq"), "chan"),
    )
    out_specs = P(("groups", "seq"), "chan")
    return jax.shard_map(
        functools.partial(shards, mesh.shape["seq"], mesh.shape["groups"]), mesh=mesh, in_specs=in_specs, out_specs=out_specs, check_vma=False)
```

```python
import functools
import math

import jax
import jax.numpy as jnp
import numpy as np
from jax import lax
from jax.experimental import pallas as pl
from jax.experimental.pallas import tpu as pltpu
from jax.sharding import PartitionSpec as P

HEAD_DIM = 128
TAPS = 128
RADIX = 128


HIGHEST = lax.Precision.HIGHEST


def shifted(value, axis, steps):
    count = lax.axis_size(axis)
    initial, last = (max(0, -steps), min(count, count - steps))
    return lax.ppermute(value, axis, [(source, source + steps) for source in range(initial, last)])


def unit_table(height, breadth, modulus, orient):
    product = (
        lax.broadcasted_iota(jnp.int32, (height, breadth), 0)
        * lax.broadcasted_iota(jnp.int32, (height, breadth), 1)
        % modulus
    )
    angles = 2.0 * math.pi / modulus * product.astype(jnp.float32)
    return (jnp.cos(angles), orient * jnp.sin(angles))


def block_table(factor, orient):
    inner_re, inner_im = unit_table(factor, factor, factor, orient)
    upper = jnp.concatenate([inner_re, inner_im], axis=1)
    lower = jnp.concatenate([-inner_im, inner_re], axis=1)
    return jnp.concatenate([upper, lower], axis=0)


def spectrum(signal, factor):
    channels, length = signal.shape
    full_length = 2 * length
    column_count = full_length // factor
    folded = signal.reshape(channels, column_count // 2, factor)
    outer_re, outer_im = unit_table(column_count, column_count // 2, column_count, -1.0)
    outer_both = jnp.concatenate([outer_re, outer_im], axis=0)
    first = jnp.einsum("kn,cnm->ckm", outer_both, folded, precision=HIGHEST)
    first_re = first[:, :column_count]
    first_im = first[:, column_count:]
    twist_re, twist_im = unit_table(column_count, factor, full_length, -1.0)
    mid_re = first_re * twist_re - first_im * twist_im
    mid_im = first_re * twist_im + first_im * twist_re
    joined = jnp.concatenate([mid_re, mid_im], axis=2)
    return jnp.einsum("ckn,nm->ckm", joined, block_table(factor, -1.0), precision=HIGHEST)


def inverse(spec_both, factor, length):
    channels = spec_both.shape[0]
    full_length = 2 * length
    column_count = full_length // factor
    mid = jnp.einsum("ckm,mn->ckn", spec_both, block_table(factor, 1.0), precision=HIGHEST)
    mid_re = mid[:, :, :factor]
    mid_im = mid[:, :, factor:]
    twist_re, twist_im = unit_table(column_count, factor, full_length, 1.0)
    turn_re = mid_re * twist_re - mid_im * twist_im
    turn_im = mid_re * twist_im + mid_im * twist_re
    outer_re, outer_im = unit_table(column_count // 2, column_count, column_count, 1.0)
    outer_both = jnp.concatenate([outer_re, -outer_im], axis=1)
    turned = jnp.concatenate([turn_re, turn_im], axis=1)
    result = jnp.einsum("nk,ckm->cnm", outer_both, turned, precision=HIGHEST)
    return result.reshape(channels, length) / full_length


def general_shards(
    gate_input, value_input, short_filter, long_filter, query_weight, key_matrix, value_matrix
):
    seq_rows, local_width = gate_input.shape
    last_rows = gate_input[seq_rows - (TAPS - 1) :]
    earlier = shifted(last_rows, "seq", 1)
    padded = jnp.concatenate([earlier, gate_input], axis=0).astype(jnp.float32)
    kernel = short_filter[:, ::-1].T[:, None, :]
    smoothed = lax.conv_general_dilated(
        padded[None],
        kernel,
        (1,),
        "VALID",
        dimension_numbers=("NHC", "HIO", "NHC"),
        feature_group_count=local_width,
        precision=HIGHEST,
    )[0]
    mixed_input = (smoothed * value_input.astype(jnp.float32)).astype(jnp.bfloat16)
    signal, kernel_line = (
        lax.all_to_all(mixed_input.T, "seq", split_axis=0, concat_axis=1, tiled=True),
        lax.all_to_all(long_filter.T, "seq", split_axis=0, concat_axis=1, tiled=True),
    )
    length = signal.shape[1]
    signal_both = spectrum(signal.astype(jnp.float32), RADIX)
    kernel_both = spectrum(kernel_line.astype(jnp.float32), RADIX)
    signal_re = signal_both[:, :, :RADIX]
    signal_im = signal_both[:, :, RADIX:]
    kernel_re = kernel_both[:, :, :RADIX]
    kernel_im = kernel_both[:, :, RADIX:]
    joint = jnp.concatenate(
        [
            signal_re * kernel_re - signal_im * kernel_im,
            signal_re * kernel_im + signal_im * kernel_re,
        ],
        axis=2,
    )
    conv_line = inverse(joint, RADIX, length).astype(jnp.bfloat16)
    my_index = lax.axis_index("seq")
    group_firsts = [my_index * seq_rows]
    conv_columns = lax.all_to_all(conv_line, "seq", split_axis=1, concat_axis=0, tiled=True)
    heads_here = local_width // HEAD_DIM
    conv_heads = conv_columns.reshape(heads_here, HEAD_DIM, seq_rows)
    query_heads = jnp.einsum(
        "hds,hde->hse", conv_heads, query_weight, preferred_element_type=jnp.float32
    ).astype(jnp.bfloat16)
    group_count = len(group_firsts)
    query_groups = [query_heads]
    key_heads = key_matrix.reshape(seq_rows, heads_here, HEAD_DIM).transpose(1, 0, 2)
    value_heads = value_matrix.reshape(seq_rows, heads_here, HEAD_DIM).transpose(1, 0, 2)
    score_scale = 1.0 / math.sqrt(HEAD_DIM)

    def attend_group(running, group_query, group_first, key_block, value_block, first_row):
        block_rows = key_block.shape[1]

        def compute(current):
            peak_value, weight_sum, weighted = current
            scores = (
                jnp.einsum(
                    "hqd,hkd->hqk", group_query, key_block, preferred_element_type=jnp.float32
                )
                * score_scale
            )
            key_pos = first_row + lax.iota(jnp.int32, block_rows)
            query_pos = group_first + lax.iota(jnp.int32, seq_rows)
            allowed = (key_pos[None, :] <= query_pos[:, None])[None]
            scores = jnp.where(allowed, scores, -1e30)
            new_peak = jnp.maximum(peak_value, jnp.max(scores, axis=2))
            weights = jnp.where(allowed, jnp.exp(scores - new_peak[:, :, None]), 0.0)
            rescale = jnp.exp(peak_value - new_peak)
            weight_sum = weight_sum * rescale + jnp.sum(weights, axis=2)
            weighted = weighted * rescale[:, :, None] + jnp.einsum(
                "hqk,hkd->hqd",
                weights.astype(jnp.bfloat16),
                value_block,
                preferred_element_type=jnp.float32,
            )
            return (new_peak, weight_sum, weighted)

        live = first_row <= group_first + seq_rows - 1
        return lax.cond(live, compute, lambda current: current, running)

    def attend(states, key_block, value_block, first_row):
        return tuple(
            (
                attend_group(
                    states[g], query_groups[g], group_firsts[g], key_block, value_block, first_row
                )
                for g in range(group_count)
            )
        )

    one_state = (
        jnp.full((heads_here, seq_rows), -1e30, jnp.float32),
        jnp.zeros((heads_here, seq_rows), jnp.float32),
        jnp.zeros((heads_here, seq_rows, HEAD_DIM), jnp.float32),
    )
    initial = tuple((one_state for g in range(group_count)))
    running = initial
    key_piece = lax.all_gather(key_heads, "seq", axis=1, tiled=True)
    value_piece = lax.all_gather(value_heads, "seq", axis=1, tiled=True)
    piece_rows = key_piece.shape[1]
    block_rows = 512
    block_count = piece_rows // block_rows
    key_blocks = key_piece.reshape(heads_here, block_count, block_rows, HEAD_DIM).transpose(
        1, 0, 2, 3
    )
    value_blocks = value_piece.reshape(heads_here, block_count, block_rows, HEAD_DIM).transpose(
        1, 0, 2, 3
    )

    def advance(current, element):
        key_block, value_block, position = element
        return (attend(current, key_block, value_block, position * block_rows), None)

    running, _ = lax.scan(
        advance, running, (key_blocks, value_blocks, lax.iota(jnp.int32, block_count))
    )
    outputs = [state[2] / state[1][:, :, None] for state in running]
    result = outputs[0]
    attended_rows = result.transpose(1, 0, 2).reshape(seq_rows, local_width).astype(jnp.bfloat16)
    return attended_rows


def split_pair(array):
    high = array.astype(jnp.bfloat16)
    return high, (array - high.astype(jnp.float32)).astype(jnp.bfloat16)


def transform_tables(rows):
    full = 2 * rows
    turn = np.arange(rows)[:, None] * np.arange(full)[None, :] % full
    angle = 2.0 * np.pi / full * turn
    forward = np.concatenate([np.cos(angle), -np.sin(angle)], axis=0)
    forward[rows] = 1.0 - 2.0 * (np.arange(full) % 2)
    weight = np.full((full,), 2.0 / full)
    weight[0] = weight[rows] = 1.0 / full
    backward = (forward[:, :rows] * weight[:, None]).T
    return forward, backward


def host_split(table):
    high = table.astype(jnp.bfloat16)
    low = (table - high.astype(np.float64)).astype(jnp.bfloat16)
    return jnp.asarray(high), jnp.asarray(low)


def dot(a, b, contract=((1,), (0,))):
    return lax.dot_general(a, b, (contract, ((), ())), preferred_element_type=jnp.float32)


GATE, VALUE, LONG, KEY, VAL = range(5)
X_LONG, X_KEY, X_VAL = range(3)
(
    LOADS,
    WEIGHTS,
    OWN_GATE,
    OWN_VALUE,
    OWN_LONG,
    OWN_LATE,
    SENT,
    SENT_PAIR,
    SENT_OUT,
    HALO,
    PAIR_EARLY,
    PAIR_LONG,
    PAIR_LATE,
    PAIR_MIXED,
    FAR_GATE,
    FAR_VALUE,
    FAR_MIXED,
    FAR_LONG,
    PASSED,
    ARRIVED,
    FAR_HEADS,
) = [*range(18), 19, 20, 21]


def block_kernel(
    count,
    gate_in,
    value_in,
    long_in,
    key_in,
    val_in,
    short_in,
    weight_in,
    table_in,
    out,
    held,
    extra,
    table,
    short_taps,
    far_taps,
    far_gate,
    far_value,
    far_before,
    far_mixed,
    head_weight,
    grid_re,
    grid_im,
    grid_nyq,
    sig_re,
    sig_im,
    mixed,
    conv,
    weights,
    sums,
    result,
    sem,
):
    me = lax.axis_index("seq")
    my_group = lax.axis_index("groups")
    rows = gate_in.shape[0]
    width = held.shape[2]
    heads = width // HEAD_DIM
    half = count // 2
    low_rows = half * rows
    share = width // lax.axis_size("groups")
    split = width // 2
    third = slice(half * rows, (half + 1) * rows)
    streams = (gate_in, value_in, long_in, key_in, val_in)
    core = lax.rem(me, 2)
    late = me // 2
    is_low = late == 0
    is_high = late == 1
    partner = me + 1 - 2 * core
    opposite = lax.rem(me + half, count)
    far = [opposite, opposite + 1 - 2 * core]
    sibling = 1 - my_group
    fwd_high = table.at[: 2 * rows]
    fwd_low = table.at[2 * rows : 4 * rows]
    inv_high = table.at[4 * rows : 5 * rows]
    inv_low = table.at[5 * rows :]

    def span(index, size):
        return pl.ds(pl.multiple_of(index * size, size), size)

    def local(source, target, slot):
        return pltpu.make_async_copy(source, target, sem.at[slot])

    def remote(source, target, send, receive, **place):
        return pltpu.make_async_remote_copy(
            src_ref=source,
            dst_ref=target,
            send_sem=sem.at[send],
            recv_sem=sem.at[receive],
            device_id=place,
            device_id_type=pl.DeviceIdType.MESH,
        )

    def wait_for(view, slot):
        local(view, view, slot).wait()

    def wait_halves(halves, slot):
        wait_for(held.at[: count, : halves * rows // (2 * count)], slot)

    far_columns = span(1 - late, 2 * width)
    my_columns = span(me, width)
    other_columns = span(opposite, width)
    my_rows = span(me, rows)
    low_block = span(core, rows)
    for source, target, slot in (
        (table_in, table, LOADS),
        (short_in.at[far_columns], far_taps, LOADS),
        (gate_in.at[:, far_columns], far_gate, LOADS),
        (value_in.at[:, far_columns], far_value, LOADS),
        (short_in.at[my_columns], short_taps, LOADS),
        (gate_in.at[:, my_columns], held.at[GATE, my_rows], OWN_GATE),
        (value_in.at[:, my_columns], held.at[VALUE, my_rows], OWN_VALUE),
        (long_in.at[:, my_columns], held.at[LONG, my_rows], OWN_LONG),
        (long_in.at[:, other_columns], extra.at[X_LONG, low_block], OWN_LONG),
        (key_in.at[:, my_columns], held.at[KEY, my_rows], OWN_LATE),
        (val_in.at[:, my_columns], held.at[VAL, my_rows], OWN_LATE),
        (key_in.at[:, other_columns], extra.at[X_KEY, low_block], OWN_LATE),
        (val_in.at[:, other_columns], extra.at[X_VAL, low_block], OWN_LATE),
        (weight_in, head_weight, WEIGHTS),
    ):
        local(source, target, slot).start()

    barrier = pltpu.get_barrier_semaphore()
    for peer in (*far, partner):
        pl.semaphore_signal(
            barrier, inc=1, device_id={"seq": peer}, device_id_type=pl.DeviceIdType.MESH
        )
    pl.semaphore_signal(
        barrier, inc=1, device_id={"groups": sibling}, device_id_type=pl.DeviceIdType.MESH
    )
    pl.semaphore_wait(barrier, count)

    my_share = pl.ds(pl.multiple_of(my_group * share, share), share)

    def share_of(peer):
        return pl.ds(pl.multiple_of(peer * width + my_group * share, share), share)

    def to_partner(a, slot):
        return remote(
            streams[a].at[:, span(partner, width)],
            held.at[a, my_rows],
            SENT,
            slot,
            seq=partner,
        )

    def extra_to_partner(a, b, slot):
        return remote(
            streams[a].at[:, span(partner + half, width)],
            extra.at[b, low_block],
            SENT_PAIR,
            slot,
            seq=partner,
        )

    def raw_to(a, peer, slot):
        return remote(
            streams[a].at[:, span(peer, width)],
            held.at[a, my_rows],
            SENT_PAIR,
            slot,
            seq=peer,
        )

    def pass_on(parity):
        source = (1 - late) * half + parity
        piece = held.at[LONG, span(source, rows), my_share]
        return remote(piece, piece, SENT, PASSED, groups=sibling)

    @pl.when(core == 0)
    def _():
        remote(
            gate_in.at[:, far_columns], far_before, SENT_PAIR, HALO, seq=partner
        ).start()

    @pl.when(me == 1)
    def _():
        remote(
            gate_in.at[:, pl.ds(width + split, split)],
            far_before.at[:, width + split :],
            SENT_PAIR,
            HALO,
            seq=half,
        ).start()

    for peer in far:
        remote(
            long_in.at[:, share_of(peer)],
            held.at[LONG, my_rows, my_share],
            SENT,
            FAR_LONG + core,
            seq=peer,
        ).start()

    @pl.when(me == 1)
    def _():
        for peer in far:
            raw_to(GATE, peer, FAR_GATE).start()

    @pl.when(me == 2)
    def _():
        raw_to(VALUE, opposite, FAR_VALUE).start()
        remote(
            value_in.at[:, width : width + split],
            held.at[VALUE, third, :split],
            SENT_PAIR,
            FAR_VALUE,
            seq=1,
        ).start()

    to_partner(GATE, PAIR_EARLY).start()
    to_partner(VALUE, PAIR_EARLY).start()
    to_partner(LONG, PAIR_LONG).start()

    @pl.when(is_low)
    def _():
        extra_to_partner(LONG, X_LONG, PAIR_LONG).start()

    wait_halves(8 * count, LOADS)

    def forward(signal):
        depth = signal.shape[0]
        both = dot(fwd_high[:, :depth], signal) + dot(fwd_low[:, :depth], signal)
        return both[:rows], both[rows:]

    def backward(re, im):
        re_high, re_low = split_pair(re)
        im_high, im_low = split_pair(im)
        high = jnp.concatenate([re_high, im_high], axis=0)
        low = jnp.concatenate([re_low, im_low], axis=0)
        return dot(inv_high[...], high) + (dot(inv_low[...], high) + dot(inv_high[...], low))

    def factor_parts(re, im):
        first = lax.broadcasted_iota(jnp.int32, re.shape, 0) == 0
        return re, jnp.where(first, 0.0, im), jnp.where(first, im, re)

    last = ((1,), (1,))

    def taps_parts(taps):
        high, low = split_pair(taps[...])
        both = dot(fwd_high[:, :TAPS], high, last) + (
            dot(fwd_low[:, :TAPS], high, last) + dot(fwd_high[:, :TAPS], low, last)
        )
        return factor_parts(both[:rows], both[rows:])

    def smooth(signal, parts):
        re, im = forward(signal)
        re_part, im_part, nyq_part = parts
        return backward(re * re_part - im * im_part, re * im_part + im * nyq_part)

    @pl.when(me == 0)
    def _():
        far_before[...] = jnp.zeros_like(far_before)

    @pl.when(me != 2)
    def _():
        far_parts = taps_parts(far_taps)

        @pl.when(core == 1)
        def _():
            wait_for(far_before, HALO)

        @pl.when(me == 3)
        def _():
            remote(
                far_before.at[:, :width], held.at[GATE, third], SENT_PAIR, FAR_GATE, seq=0
            ).start()
            remote(
                far_before.at[:, width : width + split],
                held.at[GATE, third, :split],
                SENT_PAIR,
                FAR_GATE,
                seq=1,
            ).start()

        filtered = smooth(jnp.concatenate([far_gate[...], far_before[...]], axis=0), far_parts)
        far_mixed[...] = (filtered * far_value[...].astype(jnp.float32)).astype(jnp.bfloat16)
        for peer in far:
            remote(
                far_mixed.at[:, span(lax.rem(peer, 2), width)],
                mixed.at[my_rows],
                SENT,
                FAR_MIXED,
                seq=peer,
            ).start()

    extra_mixed = span(count + core, rows)

    @pl.when(is_low)
    def _():
        remote(
            far_mixed.at[:, span(1 - core, width)],
            mixed.at[extra_mixed],
            SENT_PAIR,
            PAIR_MIXED,
            seq=partner,
        ).start()
        local(far_mixed.at[:, span(core, width)], mixed.at[extra_mixed], PAIR_MIXED).start()

    first_far = (1 - late) * half

    def send_heads(head, *arrays):
        here = head * HEAD_DIM
        for a in arrays:
            for peer in (first_far, first_far + 1):
                remote(
                    streams[a].at[:, pl.ds(pl.multiple_of(peer * width + here, HEAD_DIM), HEAD_DIM)],
                    held.at[a, my_rows, here : here + HEAD_DIM],
                    SENT,
                    FAR_HEADS + 3 * head + (0 if a == KEY else 1 + core),
                    seq=peer,
                ).start()

    send_heads(0, KEY)

    @pl.when(me == 2)
    def _():
        near = slice(width + split, 2 * width)
        near_parts = taps_parts(far_taps.at[near])
        wait_for(far_before.at[:, near], HALO)
        filtered = smooth(
            jnp.concatenate([far_gate[:, near], far_before[:, near]], axis=0), near_parts
        )
        far_mixed[:, near] = (filtered * far_value[:, near].astype(jnp.float32)).astype(
            jnp.bfloat16
        )
        remote(
            far_mixed.at[:, near], mixed.at[third, split:], SENT_PAIR, FAR_MIXED, seq=1
        ).start()

    send_heads(0, VAL)
    for head in range(1, heads):
        send_heads(head, KEY, VAL)
    to_partner(KEY, PAIR_LATE).start()
    to_partner(VAL, PAIR_LATE).start()

    @pl.when(is_low)
    def _():
        extra_to_partner(KEY, X_KEY, PAIR_LATE).start()
        extra_to_partner(VAL, X_VAL, PAIR_LATE).start()

    parts = taps_parts(short_taps)

    def rows_of(block):
        return slice(block * rows, (block + 1) * rows)

    def window(ref, block):
        now = ref[rows_of(block)]
        if block == 0:
            return now
        return jnp.concatenate([now, ref[rows_of(block - 1)]], axis=0)

    def mix(*blocks):
        for block in blocks:
            here = rows_of(block)
            filtered = smooth(window(held.at[GATE], block), parts)
            mixed[here] = (filtered * held[VALUE, here].astype(jnp.float32)).astype(jnp.bfloat16)

    def to_grid(ref, block, base=0):
        re, im, nyq = factor_parts(*forward(window(ref, block)))
        grid_re[base + block], grid_im[base + block], grid_nyq[base + block] = re, im, nyq

    def to_sig(*blocks):
        for block in blocks:
            sig_re[block], sig_im[block] = forward(mixed[rows_of(block)])

    def convolve(block, base=0):
        re = im = None
        for source in range(block + 1):
            at, lag = base + source, base + block - source
            s_re, s_im = sig_re[at], sig_im[at]
            re_term = s_re * grid_re[lag] - s_im * grid_im[lag]
            im_term = s_re * grid_im[lag] + s_im * grid_nyq[lag]
            re = re_term if re is None else re + re_term
            im = im_term if im is None else im + im_term
        conv[rows_of(base + block)] = backward(re, im).astype(jnp.bfloat16)

    def columns_of(head):
        return slice(head * HEAD_DIM, (head + 1) * HEAD_DIM)

    scale = 1.0 / math.sqrt(HEAD_DIM)

    def query(head, first, final, weight):
        here = slice(first * rows, final * rows)
        conv[here, columns_of(head)] = dot(conv[here, columns_of(head)], weight).astype(
            jnp.bfloat16
        )

    def score(head, block, keys, base=0):
        here = rows_of(base + block)
        past = (block + 1) * rows
        scores = dot(conv[here, columns_of(head)], keys[:past, columns_of(head)], last) * scale
        key_pos = lax.broadcasted_iota(jnp.int32, scores.shape, 1)
        query_pos = block * rows + lax.broadcasted_iota(jnp.int32, scores.shape, 0)
        allowed = key_pos <= query_pos
        scores = jnp.where(allowed, scores, -1e30)
        peak = jnp.max(scores, axis=1, keepdims=True)
        kept = jnp.where(allowed, jnp.exp(scores - peak), 0.0)
        sums[head, here] = jnp.broadcast_to(
            jnp.sum(kept, axis=1, keepdims=True), (rows, HEAD_DIM)
        )
        weights[head, here, :past] = kept.astype(jnp.bfloat16)

    def finish(head, block, values, base=0, owner=me):
        here = rows_of(base + block)
        past = (block + 1) * rows
        product = dot(weights[head, here, :past], values[:past, columns_of(head)])
        result[head, here] = (product / sums[head, here]).astype(jnp.bfloat16)
        source = result.at[head, here]
        target = out.at[:, pl.ds(pl.multiple_of(owner * width + head * HEAD_DIM, HEAD_DIM), HEAD_DIM)]

        @pl.when(me != block)
        def _():
            remote(source, target, SENT_OUT, ARRIVED, seq=block).start()

        @pl.when(me == block)
        def _():
            local(source, target, ARRIVED).start()

    wait_for(held.at[GATE, my_rows], OWN_GATE)
    wait_for(held.at[VALUE, my_rows], OWN_VALUE)
    wait_for(held.at[GATE, :low_rows], PAIR_EARLY)
    wait_for(held.at[LONG, :low_rows], OWN_LONG)

    @pl.when(is_low)
    def _():
        mix(0, 1)
        wait_for(held.at[LONG, :low_rows], PAIR_LONG)
        for block in range(half):
            to_grid(held.at[LONG], block)
            to_grid(extra.at[X_LONG], block, count)

    @pl.when(is_high)
    def _():
        mix(3)
        wait_for(held.at[LONG, :rows], PAIR_LONG)
        to_grid(held.at[LONG], 3)

    for parity in range(2):
        wait_for(held.at[LONG, :rows, :share], FAR_LONG + parity)
        pass_on(parity).start()

    @pl.when(is_low)
    def _():
        to_sig(0, 1)
        convolve(0)
        convolve(1)
        wait_for(held.at[LONG, :low_rows], PAIR_MIXED)
        to_sig(count, count + 1)
        convolve(0, count)
        convolve(1, count)
        wait_for(head_weight, WEIGHTS)
        wait_for(held.at[KEY], OWN_LATE)
        wait_for(held.at[KEY], PAIR_LATE)
        for head in range(heads):
            query(head, 0, half, head_weight[me * heads + head])
            query(head, count, count + half, head_weight[opposite * heads + head])
        for head in range(heads):
            for block in range(half):
                score(head, block, held.at[KEY])
                score(head, block, extra.at[X_KEY], count)
        for head in range(heads):
            for block in range(half):
                finish(head, block, held.at[VAL])
                finish(head, block, extra.at[X_VAL], count, opposite)

    @pl.when(is_high)
    def _():
        wait_for(head_weight, WEIGHTS)
        wait_for(held.at[KEY], OWN_LATE)
        wait_for(held.at[KEY, :low_rows], PAIR_LATE)

    @pl.when(me == 0)
    def _():
        wait_for(held.at[VALUE, :rows], FAR_VALUE)

    @pl.when(me == 1)
    def _():
        wait_for(held.at[VALUE, third, :split], FAR_VALUE)
        wait_for(held.at[GATE, third, :split], FAR_GATE)
        signal = window(held.at[GATE, :, :split], 2)
        filtered = smooth(signal, [part[:, :split] for part in parts])
        mixed[third, :split] = (filtered * held[VALUE, third, :split].astype(jnp.float32)).astype(
            jnp.bfloat16
        )

    @pl.when(me != 1)
    def _():
        wait_for(held.at[GATE, :rows], FAR_GATE)
        mix(2)

    wait_for(held.at[LONG, :low_rows, :share], PASSED)

    @pl.when(is_low)
    def _():
        to_grid(held.at[LONG], 3)

    @pl.when(is_high)
    def _():
        for block in range(half):
            to_grid(held.at[LONG], block)
        to_sig(3)

    to_grid(held.at[LONG], 2)

    @pl.when(me == 0)
    def _():
        wait_for(mixed.at[:rows], FAR_MIXED)

    @pl.when(me == 1)
    def _():
        wait_for(mixed.at[: rows + rows // 2], FAR_MIXED)

    @pl.when(is_high)
    def _():
        wait_for(mixed.at[:low_rows], FAR_MIXED)

    @pl.when(is_low)
    def _():
        to_sig(3)

    @pl.when(is_high)
    def _():
        to_sig(0, 1)

    to_sig(2)
    convolve(2)
    convolve(3)
    for head in range(heads):
        query(head, half, count, head_weight[me * heads + head])
        first = FAR_HEADS + 3 * head
        wait_for(held.at[KEY, :low_rows, columns_of(head)], first)
        score(head, 2, held.at[KEY])
        score(head, 3, held.at[KEY])
        wait_for(held.at[VAL, :rows, columns_of(head)], first + 1)

        @pl.when(is_high)
        def _():
            wait_for(held.at[VAL, :rows, columns_of(head)], first + 2)

        finish(head, 2, held.at[VAL])

        @pl.when(is_low)
        def _():
            wait_for(held.at[VAL, :rows, columns_of(head)], first + 2)

        finish(head, 3, held.at[VAL])

    @pl.when(me == 2)
    def _():
        wait_halves(22, SENT)
        wait_halves(8, SENT_PAIR)

    @pl.when(me != 2)
    def _():
        wait_halves(26, SENT)

    @pl.when(me == 3)
    def _():
        wait_halves(3, SENT_PAIR)

    @pl.when(me == 0)
    def _():
        wait_halves(12, SENT_PAIR)

    @pl.when(me == 1)
    def _():
        wait_halves(13, SENT_PAIR)

    @pl.when(is_low)
    def _():
        wait_halves(8, SENT_OUT)

    @pl.when(is_high)
    def _():
        wait_halves(2, SENT_OUT)

    wait_for(out, ARRIVED)


def head_shards(
    count,
    gate_input,
    value_input,
    short_filter,
    long_filter,
    query_weight,
    key_matrix,
    value_matrix,
):
    rows, local_width = gate_input.shape
    width = local_width // count
    heads = width // HEAD_DIM
    length = count * rows
    blocks = count + count // 2
    both_rows = blocks * rows
    forward, inverse_table = transform_tables(rows)
    table = jnp.concatenate([*host_split(forward), *host_split(inverse_table)], axis=0)
    bf16, f32 = jnp.bfloat16, jnp.float32
    return pl.pallas_call(
        functools.partial(block_kernel, count),
        out_shape=pltpu.VMEM((rows, local_width), bf16),
        in_specs=[pl.BlockSpec(memory_space=pl.ANY)] * 8,
        out_specs=pl.BlockSpec(memory_space=pltpu.VMEM),
        scratch_shapes=[
            pltpu.VMEM((5, length, width), bf16),
            pltpu.VMEM((3, length // 2, width), bf16),
            pltpu.VMEM((6 * rows, 2 * rows), bf16),
            pltpu.VMEM((width, TAPS), f32),
            pltpu.VMEM((2 * width, TAPS), f32),
            pltpu.VMEM((rows, 2 * width), bf16),
            pltpu.VMEM((rows, 2 * width), bf16),
            pltpu.VMEM((rows, 2 * width), bf16),
            pltpu.VMEM((rows, 2 * width), bf16),
            pltpu.VMEM(query_weight.shape, bf16),
            pltpu.VMEM((blocks, rows, width), f32),
            pltpu.VMEM((blocks, rows, width), f32),
            pltpu.VMEM((blocks, rows, width), f32),
            pltpu.VMEM((blocks, rows, width), f32),
            pltpu.VMEM((blocks, rows, width), f32),
            pltpu.VMEM((both_rows, width), bf16),
            pltpu.VMEM((both_rows, width), bf16),
            pltpu.VMEM((heads, both_rows, length), bf16),
            pltpu.VMEM((heads, both_rows, HEAD_DIM), f32),
            pltpu.VMEM((heads, both_rows, HEAD_DIM), bf16),
            pltpu.SemaphoreType.DMA((FAR_HEADS + 3 * heads,)),
        ],
        compiler_params=pltpu.CompilerParams(
            collective_id=0,
            has_side_effects=True,
        ),
    )(
        gate_input,
        value_input,
        long_filter,
        key_matrix,
        value_matrix,
        short_filter,
        query_weight,
        table,
    )


def shards(count, groups, gate_input, *others):
    rows, local_width = gate_input.shape
    by_heads = local_width % (count * groups * HEAD_DIM) == 0
    by_rows = rows >= TAPS and rows % HEAD_DIM == 0
    two_pairs = count == 4 and groups == 2
    if two_pairs and by_heads and by_rows:
        return head_shards(count, gate_input, *others)
    return general_shards(gate_input, *others)


def solution(mesh):
    in_specs = (
        P(("groups", "seq"), "chan"),
        P(("groups", "seq"), "chan"),
        P("chan", None),
        P("seq", "chan"),
        P("chan", None, None),
        P(("groups", "seq"), "chan"),
        P(("groups", "seq"), "chan"),
    )
    out_specs = P(("groups", "seq"), "chan")
    return jax.shard_map(
        functools.partial(shards, mesh.shape["seq"], mesh.shape["groups"]), mesh=mesh, in_specs=in_specs, out_specs=out_specs, check_vma=False)
```

```python
import functools
import math

import jax
import jax.numpy as jnp
import numpy as np
from jax import lax
from jax.experimental import pallas as pl
from jax.experimental.pallas import tpu as pltpu
from jax.sharding import PartitionSpec as P

HEAD_DIM = 128
TAPS = 128
RADIX = 128


HIGHEST = lax.Precision.HIGHEST


def shifted(value, axis, steps):
    count = lax.axis_size(axis)
    initial, last = (max(0, -steps), min(count, count - steps))
    return lax.ppermute(value, axis, [(source, source + steps) for source in range(initial, last)])


def unit_table(height, breadth, modulus, orient):
    product = (
        lax.broadcasted_iota(jnp.int32, (height, breadth), 0)
        * lax.broadcasted_iota(jnp.int32, (height, breadth), 1)
        % modulus
    )
    angles = 2.0 * math.pi / modulus * product.astype(jnp.float32)
    return (jnp.cos(angles), orient * jnp.sin(angles))


def block_table(factor, orient):
    inner_re, inner_im = unit_table(factor, factor, factor, orient)
    upper = jnp.concatenate([inner_re, inner_im], axis=1)
    lower = jnp.concatenate([-inner_im, inner_re], axis=1)
    return jnp.concatenate([upper, lower], axis=0)


def spectrum(signal, factor):
    channels, length = signal.shape
    full_length = 2 * length
    column_count = full_length // factor
    folded = signal.reshape(channels, column_count // 2, factor)
    outer_re, outer_im = unit_table(column_count, column_count // 2, column_count, -1.0)
    outer_both = jnp.concatenate([outer_re, outer_im], axis=0)
    first = jnp.einsum("kn,cnm->ckm", outer_both, folded, precision=HIGHEST)
    first_re = first[:, :column_count]
    first_im = first[:, column_count:]
    twist_re, twist_im = unit_table(column_count, factor, full_length, -1.0)
    mid_re = first_re * twist_re - first_im * twist_im
    mid_im = first_re * twist_im + first_im * twist_re
    joined = jnp.concatenate([mid_re, mid_im], axis=2)
    return jnp.einsum("ckn,nm->ckm", joined, block_table(factor, -1.0), precision=HIGHEST)


def inverse(spec_both, factor, length):
    channels = spec_both.shape[0]
    full_length = 2 * length
    column_count = full_length // factor
    mid = jnp.einsum("ckm,mn->ckn", spec_both, block_table(factor, 1.0), precision=HIGHEST)
    mid_re = mid[:, :, :factor]
    mid_im = mid[:, :, factor:]
    twist_re, twist_im = unit_table(column_count, factor, full_length, 1.0)
    turn_re = mid_re * twist_re - mid_im * twist_im
    turn_im = mid_re * twist_im + mid_im * twist_re
    outer_re, outer_im = unit_table(column_count // 2, column_count, column_count, 1.0)
    outer_both = jnp.concatenate([outer_re, -outer_im], axis=1)
    turned = jnp.concatenate([turn_re, turn_im], axis=1)
    result = jnp.einsum("nk,ckm->cnm", outer_both, turned, precision=HIGHEST)
    return result.reshape(channels, length) / full_length


def general_shards(
    gate_input, value_input, short_filter, long_filter, query_weight, key_matrix, value_matrix
):
    seq_rows, local_width = gate_input.shape
    last_rows = gate_input[seq_rows - (TAPS - 1) :]
    earlier = shifted(last_rows, "seq", 1)
    padded = jnp.concatenate([earlier, gate_input], axis=0).astype(jnp.float32)
    kernel = short_filter[:, ::-1].T[:, None, :]
    smoothed = lax.conv_general_dilated(
        padded[None],
        kernel,
        (1,),
        "VALID",
        dimension_numbers=("NHC", "HIO", "NHC"),
        feature_group_count=local_width,
        precision=HIGHEST,
    )[0]
    mixed_input = (smoothed * value_input.astype(jnp.float32)).astype(jnp.bfloat16)
    signal, kernel_line = (
        lax.all_to_all(mixed_input.T, "seq", split_axis=0, concat_axis=1, tiled=True),
        lax.all_to_all(long_filter.T, "seq", split_axis=0, concat_axis=1, tiled=True),
    )
    length = signal.shape[1]
    signal_both = spectrum(signal.astype(jnp.float32), RADIX)
    kernel_both = spectrum(kernel_line.astype(jnp.float32), RADIX)
    signal_re = signal_both[:, :, :RADIX]
    signal_im = signal_both[:, :, RADIX:]
    kernel_re = kernel_both[:, :, :RADIX]
    kernel_im = kernel_both[:, :, RADIX:]
    joint = jnp.concatenate(
        [
            signal_re * kernel_re - signal_im * kernel_im,
            signal_re * kernel_im + signal_im * kernel_re,
        ],
        axis=2,
    )
    conv_line = inverse(joint, RADIX, length).astype(jnp.bfloat16)
    my_index = lax.axis_index("seq")
    group_firsts = [my_index * seq_rows]
    conv_columns = lax.all_to_all(conv_line, "seq", split_axis=1, concat_axis=0, tiled=True)
    heads_here = local_width // HEAD_DIM
    conv_heads = conv_columns.reshape(heads_here, HEAD_DIM, seq_rows)
    query_heads = jnp.einsum(
        "hds,hde->hse", conv_heads, query_weight, preferred_element_type=jnp.float32
    ).astype(jnp.bfloat16)
    group_count = len(group_firsts)
    query_groups = [query_heads]
    key_heads = key_matrix.reshape(seq_rows, heads_here, HEAD_DIM).transpose(1, 0, 2)
    value_heads = value_matrix.reshape(seq_rows, heads_here, HEAD_DIM).transpose(1, 0, 2)
    score_scale = 1.0 / math.sqrt(HEAD_DIM)

    def attend_group(running, group_query, group_first, key_block, value_block, first_row):
        block_rows = key_block.shape[1]

        def compute(current):
            peak_value, weight_sum, weighted = current
            scores = (
                jnp.einsum(
                    "hqd,hkd->hqk", group_query, key_block, preferred_element_type=jnp.float32
                )
                * score_scale
            )
            key_pos = first_row + lax.iota(jnp.int32, block_rows)
            query_pos = group_first + lax.iota(jnp.int32, seq_rows)
            allowed = (key_pos[None, :] <= query_pos[:, None])[None]
            scores = jnp.where(allowed, scores, -1e30)
            new_peak = jnp.maximum(peak_value, jnp.max(scores, axis=2))
            weights = jnp.where(allowed, jnp.exp(scores - new_peak[:, :, None]), 0.0)
            rescale = jnp.exp(peak_value - new_peak)
            weight_sum = weight_sum * rescale + jnp.sum(weights, axis=2)
            weighted = weighted * rescale[:, :, None] + jnp.einsum(
                "hqk,hkd->hqd",
                weights.astype(jnp.bfloat16),
                value_block,
                preferred_element_type=jnp.float32,
            )
            return (new_peak, weight_sum, weighted)

        live = first_row <= group_first + seq_rows - 1
        return lax.cond(live, compute, lambda current: current, running)

    def attend(states, key_block, value_block, first_row):
        return tuple(
            (
                attend_group(
                    states[g], query_groups[g], group_firsts[g], key_block, value_block, first_row
                )
                for g in range(group_count)
            )
        )

    one_state = (
        jnp.full((heads_here, seq_rows), -1e30, jnp.float32),
        jnp.zeros((heads_here, seq_rows), jnp.float32),
        jnp.zeros((heads_here, seq_rows, HEAD_DIM), jnp.float32),
    )
    initial = tuple((one_state for g in range(group_count)))
    running = initial
    key_piece = lax.all_gather(key_heads, "seq", axis=1, tiled=True)
    value_piece = lax.all_gather(value_heads, "seq", axis=1, tiled=True)
    piece_rows = key_piece.shape[1]
    block_rows = 512
    block_count = piece_rows // block_rows
    key_blocks = key_piece.reshape(heads_here, block_count, block_rows, HEAD_DIM).transpose(
        1, 0, 2, 3
    )
    value_blocks = value_piece.reshape(heads_here, block_count, block_rows, HEAD_DIM).transpose(
        1, 0, 2, 3
    )

    def advance(current, element):
        key_block, value_block, position = element
        return (attend(current, key_block, value_block, position * block_rows), None)

    running, _ = lax.scan(
        advance, running, (key_blocks, value_blocks, lax.iota(jnp.int32, block_count))
    )
    outputs = [state[2] / state[1][:, :, None] for state in running]
    result = outputs[0]
    attended_rows = result.transpose(1, 0, 2).reshape(seq_rows, local_width).astype(jnp.bfloat16)
    return attended_rows


def split_pair(array):
    high = array.astype(jnp.bfloat16)
    return high, (array - high.astype(jnp.float32)).astype(jnp.bfloat16)


def transform_tables(rows):
    full = 2 * rows
    turn = np.arange(rows)[:, None] * np.arange(full)[None, :] % full
    angle = 2.0 * np.pi / full * turn
    forward = np.concatenate([np.cos(angle), -np.sin(angle)], axis=0)
    forward[rows] = 1.0 - 2.0 * (np.arange(full) % 2)
    weight = np.full((full,), 2.0 / full)
    weight[0] = weight[rows] = 1.0 / full
    backward = (forward[:, :rows] * weight[:, None]).T
    return forward, backward


def host_split(table):
    high = table.astype(jnp.bfloat16)
    low = (table - high.astype(np.float64)).astype(jnp.bfloat16)
    return jnp.asarray(high), jnp.asarray(low)


def dot(a, b, contract=((1,), (0,))):
    return lax.dot_general(a, b, (contract, ((), ())), preferred_element_type=jnp.float32)


GATE, VALUE, LONG, KEY, VAL = range(5)
X_LONG, X_KEY, X_VAL = range(3)
(
    LOADS,
    OWN,
    SENT,
    SENT_PAIR,
    SENT_OUT,
    HALO,
    PAIR_EARLY,
    PAIR_LONG,
    PAIR_LATE,
    PAIR_MIXED,
    FAR_GATE,
    FAR_VALUE,
    FAR_MIXED,
    FAR_LONG,
    PASSED,
    ARRIVED,
    FAR_HEADS,
) = [*range(14), 15, 16, 17]


def block_kernel(
    count,
    gate_in,
    value_in,
    long_in,
    key_in,
    val_in,
    short_in,
    weight_in,
    table_in,
    out,
    held,
    extra,
    table,
    short_taps,
    far_taps,
    far_gate,
    far_value,
    far_before,
    far_mixed,
    head_weight,
    grid_re,
    grid_im,
    grid_nyq,
    sig_re,
    sig_im,
    mixed,
    conv,
    weights,
    sums,
    result,
    sem,
):
    me = lax.axis_index("seq")
    my_group = lax.axis_index("groups")
    rows = gate_in.shape[0]
    width = held.shape[2]
    heads = width // HEAD_DIM
    half = count // 2
    low_rows = half * rows
    share = width // lax.axis_size("groups")
    split = width // 2
    third = slice(half * rows, (half + 1) * rows)
    streams = (gate_in, value_in, long_in, key_in, val_in)
    core = lax.rem(me, 2)
    late = me // 2
    is_low = late == 0
    is_high = late == 1
    partner = me + 1 - 2 * core
    opposite = lax.rem(me + half, count)
    far = [opposite, opposite + 1 - 2 * core]
    sibling = 1 - my_group
    first_far = (1 - late) * half
    fwd_high = table.at[: 2 * rows]
    fwd_low = table.at[2 * rows : 4 * rows]
    inv_high = table.at[4 * rows : 5 * rows]
    inv_low = table.at[5 * rows :]

    def span(index, size):
        return pl.ds(pl.multiple_of(index * size, size), size)

    def local(source, target, slot):
        return pltpu.make_async_copy(source, target, sem.at[slot])

    def remote(source, target, send, receive, **place):
        return pltpu.make_async_remote_copy(
            src_ref=source,
            dst_ref=target,
            send_sem=sem.at[send],
            recv_sem=sem.at[receive],
            device_id=place,
            device_id_type=pl.DeviceIdType.MESH,
        )

    def wait_for(view, slot):
        local(view, view, slot).wait()

    def wait_halves(halves, slot):
        wait_for(held.at[: count, : halves * rows // (2 * count)], slot)

    far_columns = span(1 - late, 2 * width)
    my_columns = span(me, width)
    other_columns = span(opposite, width)
    my_rows = span(me, rows)
    low_block = span(core, rows)
    for source, target, slot in (
        (table_in, table, LOADS),
        (short_in.at[far_columns], far_taps, LOADS),
        (gate_in.at[:, far_columns], far_gate, LOADS),
        (value_in.at[:, far_columns], far_value, LOADS),
        (short_in.at[my_columns], short_taps, LOADS),
        (gate_in.at[:, my_columns], held.at[GATE, my_rows], OWN),
        (value_in.at[:, my_columns], held.at[VALUE, my_rows], OWN),
        (long_in.at[:, my_columns], held.at[LONG, my_rows], OWN),
        (long_in.at[:, other_columns], extra.at[X_LONG, low_block], OWN),
        (key_in.at[:, my_columns], held.at[KEY, my_rows], OWN),
        (val_in.at[:, my_columns], held.at[VAL, my_rows], OWN),
        (key_in.at[:, other_columns], extra.at[X_KEY, low_block], OWN),
        (val_in.at[:, other_columns], extra.at[X_VAL, low_block], OWN),
        (weight_in, head_weight, OWN),
    ):
        local(source, target, slot).start()

    barrier = pltpu.get_barrier_semaphore()
    for peer in (*far, partner):
        pl.semaphore_signal(
            barrier, inc=1, device_id={"seq": peer}, device_id_type=pl.DeviceIdType.MESH
        )
    pl.semaphore_signal(
        barrier, inc=1, device_id={"groups": sibling}, device_id_type=pl.DeviceIdType.MESH
    )
    pl.semaphore_wait(barrier, count)

    my_share = pl.ds(pl.multiple_of(my_group * share, share), share)

    def share_of(peer):
        return pl.ds(pl.multiple_of(peer * width + my_group * share, share), share)

    def to_partner(a, slot):
        return remote(
            streams[a].at[:, span(partner, width)],
            held.at[a, my_rows],
            SENT,
            slot,
            seq=partner,
        )

    def extra_to_partner(a, b, slot):
        return remote(
            streams[a].at[:, span(partner + half, width)],
            extra.at[b, low_block],
            SENT_PAIR,
            slot,
            seq=partner,
        )

    def raw_to(a, peer, slot):
        return remote(
            streams[a].at[:, span(peer, width)],
            held.at[a, my_rows],
            SENT_PAIR,
            slot,
            seq=peer,
        )

    def pass_on(parity):
        source = (1 - late) * half + parity
        piece = held.at[LONG, span(source, rows), my_share]
        return remote(piece, piece, SENT, PASSED, groups=sibling)

    @pl.when(core == 0)
    def _():
        remote(
            gate_in.at[:, far_columns], far_before, SENT_PAIR, HALO, seq=partner
        ).start()

    @pl.when(me == 1)
    def _():
        remote(
            gate_in.at[:, pl.ds(width + split, split)],
            far_before.at[:, width + split :],
            SENT_PAIR,
            HALO,
            seq=half,
        ).start()

    for peer in far:
        remote(
            long_in.at[:, share_of(peer)],
            held.at[LONG, my_rows, my_share],
            SENT,
            FAR_LONG + core,
            seq=peer,
        ).start()

    @pl.when(me == 1)
    def _():
        for peer in far:
            raw_to(GATE, peer, FAR_GATE).start()

    @pl.when(me == 2)
    def _():
        raw_to(VALUE, opposite, FAR_VALUE).start()
        for stream, a, slot in ((gate_in, GATE, FAR_GATE), (value_in, VALUE, FAR_VALUE)):
            remote(
                stream.at[:, width : width + split],
                held.at[a, third, :split],
                SENT_PAIR,
                slot,
                seq=1,
            ).start()

    to_partner(GATE, PAIR_EARLY).start()
    to_partner(VALUE, PAIR_EARLY).start()
    to_partner(LONG, PAIR_LONG).start()

    @pl.when(is_low)
    def _():
        extra_to_partner(LONG, X_LONG, PAIR_LONG).start()

    def send_head(head, a, peer):
        here = head * HEAD_DIM
        remote(
            streams[a].at[:, pl.ds(pl.multiple_of(peer * width + here, HEAD_DIM), HEAD_DIM)],
            held.at[a, my_rows, here : here + HEAD_DIM],
            SENT,
            FAR_HEADS + 3 * head + (0 if a == KEY else 1 + core),
            seq=peer,
        ).start()

    def send_heads(head, *arrays):
        for a in arrays:
            for index in range(half):
                send_head(head, a, first_far + index)

    @pl.when(is_high)
    def _():
        send_heads(0, KEY)

    wait_halves(8 * count, LOADS)

    def forward(signal):
        depth = signal.shape[0]
        both = dot(fwd_high[:, :depth], signal) + dot(fwd_low[:, :depth], signal)
        return both[:rows], both[rows:]

    def backward(re, im):
        re_high, re_low = split_pair(re)
        im_high, im_low = split_pair(im)
        high = jnp.concatenate([re_high, im_high], axis=0)
        low = jnp.concatenate([re_low, im_low], axis=0)
        return dot(inv_high[...], high) + (dot(inv_low[...], high) + dot(inv_high[...], low))

    def factor_parts(re, im):
        first = lax.broadcasted_iota(jnp.int32, re.shape, 0) == 0
        return re, jnp.where(first, 0.0, im), jnp.where(first, im, re)

    last = ((1,), (1,))

    def taps_parts(taps):
        high, low = split_pair(taps[...])
        both = dot(fwd_high[:, :TAPS], high, last) + (
            dot(fwd_low[:, :TAPS], high, last) + dot(fwd_high[:, :TAPS], low, last)
        )
        return factor_parts(both[:rows], both[rows:])

    def smooth(signal, parts):
        re, im = forward(signal)
        re_part, im_part, nyq_part = parts
        return backward(re * re_part - im * im_part, re * im_part + im * nyq_part)

    @pl.when(me == 0)
    def _():
        far_before[...] = jnp.zeros_like(far_before)

    @pl.when(me != 2)
    def _():
        far_parts = taps_parts(far_taps)

        @pl.when(core == 1)
        def _():
            wait_for(far_before, HALO)

        @pl.when(me == 3)
        def _():
            remote(
                far_before.at[:, :width], held.at[GATE, third], SENT_PAIR, FAR_GATE, seq=0
            ).start()

        filtered = smooth(jnp.concatenate([far_gate[...], far_before[...]], axis=0), far_parts)
        far_mixed[...] = (filtered * far_value[...].astype(jnp.float32)).astype(jnp.bfloat16)
        for parity in range(half):
            peer = first_far + parity
            remote(
                far_mixed.at[:, parity * width : (parity + 1) * width],
                mixed.at[my_rows],
                SENT,
                FAR_MIXED,
                seq=peer,
            ).start()

    extra_mixed = span(count + core, rows)

    @pl.when(is_low)
    def _():
        remote(
            far_mixed.at[:, span(1 - core, width)],
            mixed.at[extra_mixed],
            SENT_PAIR,
            PAIR_MIXED,
            seq=partner,
        ).start()
        local(far_mixed.at[:, span(core, width)], mixed.at[extra_mixed], PAIR_MIXED).start()

    @pl.when(is_low)
    def _():
        send_heads(0, KEY)

    @pl.when(me == 2)
    def _():
        near = slice(width + split, 2 * width)
        near_parts = taps_parts(far_taps.at[near])
        wait_for(far_before.at[:, near], HALO)
        filtered = smooth(
            jnp.concatenate([far_gate[:, near], far_before[:, near]], axis=0), near_parts
        )
        far_mixed[:, near] = (filtered * far_value[:, near].astype(jnp.float32)).astype(
            jnp.bfloat16
        )
        remote(
            far_mixed.at[:, near], mixed.at[third, split:], SENT_PAIR, FAR_MIXED, seq=1
        ).start()

    send_heads(0, VAL)
    @pl.when(is_low)
    def _():
        for head in range(1, heads):
            send_heads(head, KEY, VAL)

    @pl.when(is_high)
    def _():
        for head in range(1, heads):
            for index in range(half):
                for a in (KEY, VAL):
                    send_head(head, a, index)

    to_partner(KEY, PAIR_LATE).start()
    to_partner(VAL, PAIR_LATE).start()

    @pl.when(is_low)
    def _():
        extra_to_partner(KEY, X_KEY, PAIR_LATE).start()
        extra_to_partner(VAL, X_VAL, PAIR_LATE).start()

    parts = taps_parts(short_taps)

    def rows_of(block):
        return slice(block * rows, (block + 1) * rows)

    def window(ref, block):
        now = ref[rows_of(block)]
        if block == 0:
            return now
        return jnp.concatenate([now, ref[rows_of(block - 1)]], axis=0)

    def mix(*blocks):
        for block in blocks:
            here = rows_of(block)
            filtered = smooth(window(held.at[GATE], block), parts)
            mixed[here] = (filtered * held[VALUE, here].astype(jnp.float32)).astype(jnp.bfloat16)

    def to_grid(ref, block, base=0):
        re, im, nyq = factor_parts(*forward(window(ref, block)))
        grid_re[base + block], grid_im[base + block], grid_nyq[base + block] = re, im, nyq

    def to_sig(*blocks):
        for block in blocks:
            sig_re[block], sig_im[block] = forward(mixed[rows_of(block)])

    def convolve(block, base=0):
        re = im = None
        for source in range(block + 1):
            at, lag = base + source, base + block - source
            s_re, s_im = sig_re[at], sig_im[at]
            re_term = s_re * grid_re[lag] - s_im * grid_im[lag]
            im_term = s_re * grid_im[lag] + s_im * grid_nyq[lag]
            re = re_term if re is None else re + re_term
            im = im_term if im is None else im + im_term
        conv[rows_of(base + block)] = backward(re, im).astype(jnp.bfloat16)

    def columns_of(head):
        return slice(head * HEAD_DIM, (head + 1) * HEAD_DIM)

    scale = 1.0 / math.sqrt(HEAD_DIM)

    def query(head, first, final, weight):
        here = slice(first * rows, final * rows)
        conv[here, columns_of(head)] = dot(conv[here, columns_of(head)], weight).astype(
            jnp.bfloat16
        )

    def score(head, block, keys, base=0):
        here = rows_of(base + block)
        past = (block + 1) * rows
        scores = dot(conv[here, columns_of(head)], keys[:past, columns_of(head)], last) * scale
        key_pos = lax.broadcasted_iota(jnp.int32, scores.shape, 1)
        query_pos = block * rows + lax.broadcasted_iota(jnp.int32, scores.shape, 0)
        allowed = key_pos <= query_pos
        scores = jnp.where(allowed, scores, -1e30)
        peak = jnp.max(scores, axis=1, keepdims=True)
        kept = jnp.where(allowed, jnp.exp(scores - peak), 0.0)
        sums[head, here] = jnp.broadcast_to(
            jnp.sum(kept, axis=1, keepdims=True), (rows, HEAD_DIM)
        )
        weights[head, here, :past] = kept.astype(jnp.bfloat16)

    def finish(head, block, values, base=0, owner=me):
        here = rows_of(base + block)
        past = (block + 1) * rows
        product = dot(weights[head, here, :past], values[:past, columns_of(head)])
        result[head, here] = (product / sums[head, here]).astype(jnp.bfloat16)
        source = result.at[head, here]
        target = out.at[:, pl.ds(pl.multiple_of(owner * width + head * HEAD_DIM, HEAD_DIM), HEAD_DIM)]

        @pl.when(me != block)
        def _():
            remote(source, target, SENT_OUT, ARRIVED, seq=block).start()

        @pl.when(me == block)
        def _():
            local(source, target, ARRIVED).start()

    wait_for(held.at[:3, :], OWN)
    wait_for(held.at[GATE, :low_rows], PAIR_EARLY)

    @pl.when(is_low)
    def _():
        mix(0, 1)
        wait_for(held.at[LONG, :low_rows], PAIR_LONG)
        for block in range(half):
            to_grid(held.at[LONG], block)
            to_grid(extra.at[X_LONG], block, count)

    @pl.when(is_high)
    def _():
        mix(3)
        wait_for(held.at[LONG, :rows], PAIR_LONG)
        to_grid(held.at[LONG], 3)

    for parity in range(2):
        wait_for(held.at[LONG, :rows, :share], FAR_LONG + parity)
        pass_on(parity).start()

    @pl.when(is_low)
    def _():
        to_sig(0, 1)
        convolve(0)
        convolve(1)
        wait_for(held.at[LONG, :low_rows], PAIR_MIXED)
        to_sig(count, count + 1)
        convolve(0, count)
        convolve(1, count)
        wait_for(held.at[KEY], PAIR_LATE)
        for head in range(heads):
            query(head, 0, half, head_weight[me * heads + head])
            query(head, count, count + half, head_weight[opposite * heads + head])
        for head in range(heads):
            for block in range(half):
                score(head, block, held.at[KEY])
                score(head, block, extra.at[X_KEY], count)
        for head in range(heads):
            for block in range(half):
                finish(head, block, held.at[VAL])
                finish(head, block, extra.at[X_VAL], count, opposite)

    @pl.when(is_high)
    def _():
        wait_for(held.at[KEY, :low_rows], PAIR_LATE)

    @pl.when(me == 0)
    def _():
        wait_for(held.at[VALUE, :rows], FAR_VALUE)

    @pl.when(me == 1)
    def _():
        wait_for(held.at[VALUE, third, :split], FAR_VALUE)
        wait_for(held.at[GATE, third, :split], FAR_GATE)
        signal = window(held.at[GATE, :, :split], 2)
        filtered = smooth(signal, [part[:, :split] for part in parts])
        mixed[third, :split] = (filtered * held[VALUE, third, :split].astype(jnp.float32)).astype(
            jnp.bfloat16
        )

    @pl.when(me != 1)
    def _():
        wait_for(held.at[GATE, :rows], FAR_GATE)
        mix(2)

    wait_for(held.at[LONG, :low_rows, :share], PASSED)

    @pl.when(is_low)
    def _():
        to_grid(held.at[LONG], 3)

    @pl.when(is_high)
    def _():
        for block in range(half):
            to_grid(held.at[LONG], block)
        to_sig(3)

    to_grid(held.at[LONG], 2)

    @pl.when(me == 0)
    def _():
        wait_for(mixed.at[:rows], FAR_MIXED)

    @pl.when(me == 1)
    def _():
        wait_for(mixed.at[: rows + rows // 2], FAR_MIXED)

    @pl.when(is_high)
    def _():
        wait_for(mixed.at[:low_rows], FAR_MIXED)

    @pl.when(is_low)
    def _():
        to_sig(3)

    @pl.when(is_high)
    def _():
        to_sig(0, 1)

    to_sig(2)
    convolve(2)
    convolve(3)
    for head in range(heads):
        query(head, half, count, head_weight[me * heads + head])
        first = FAR_HEADS + 3 * head
        wait_for(held.at[KEY, :low_rows, columns_of(head)], first)
        score(head, 2, held.at[KEY])
        score(head, 3, held.at[KEY])
        wait_for(held.at[VAL, :rows, columns_of(head)], first + 1)

        @pl.when(is_high)
        def _():
            wait_for(held.at[VAL, :rows, columns_of(head)], first + 2)

        finish(head, 2, held.at[VAL])

        @pl.when(is_low)
        def _():
            wait_for(held.at[VAL, :rows, columns_of(head)], first + 2)

        finish(head, 3, held.at[VAL])

    @pl.when(me == 2)
    def _():
        wait_halves(22, SENT)
        wait_halves(9, SENT_PAIR)

    @pl.when(me != 2)
    def _():
        wait_halves(26, SENT)

    @pl.when(me == 3)
    def _():
        wait_halves(2, SENT_PAIR)

    @pl.when(me == 0)
    def _():
        wait_halves(12, SENT_PAIR)

    @pl.when(me == 1)
    def _():
        wait_halves(13, SENT_PAIR)

    @pl.when(is_low)
    def _():
        wait_halves(8, SENT_OUT)

    @pl.when(is_high)
    def _():
        wait_halves(2, SENT_OUT)

    wait_for(out, ARRIVED)


def head_shards(
    count,
    gate_input,
    value_input,
    short_filter,
    long_filter,
    query_weight,
    key_matrix,
    value_matrix,
):
    rows, local_width = gate_input.shape
    width = local_width // count
    heads = width // HEAD_DIM
    length = count * rows
    blocks = count + count // 2
    both_rows = blocks * rows
    forward, inverse_table = transform_tables(rows)
    table = jnp.concatenate([*host_split(forward), *host_split(inverse_table)], axis=0)
    bf16, f32 = jnp.bfloat16, jnp.float32
    return pl.pallas_call(
        functools.partial(block_kernel, count),
        out_shape=pltpu.VMEM((rows, local_width), bf16),
        in_specs=[pl.BlockSpec(memory_space=pl.ANY)] * 8,
        out_specs=pl.BlockSpec(memory_space=pltpu.VMEM),
        scratch_shapes=[
            pltpu.VMEM((5, length, width), bf16),
            pltpu.VMEM((3, length // 2, width), bf16),
            pltpu.VMEM((6 * rows, 2 * rows), bf16),
            pltpu.VMEM((width, TAPS), f32),
            pltpu.VMEM((2 * width, TAPS), f32),
            pltpu.VMEM((rows, 2 * width), bf16),
            pltpu.VMEM((rows, 2 * width), bf16),
            pltpu.VMEM((rows, 2 * width), bf16),
            pltpu.VMEM((rows, 2 * width), bf16),
            pltpu.VMEM(query_weight.shape, bf16),
            pltpu.VMEM((blocks, rows, width), f32),
            pltpu.VMEM((blocks, rows, width), f32),
            pltpu.VMEM((blocks, rows, width), f32),
            pltpu.VMEM((blocks, rows, width), f32),
            pltpu.VMEM((blocks, rows, width), f32),
            pltpu.VMEM((both_rows, width), bf16),
            pltpu.VMEM((both_rows, width), bf16),
            pltpu.VMEM((heads, both_rows, length), bf16),
            pltpu.VMEM((heads, both_rows, HEAD_DIM), f32),
            pltpu.VMEM((heads, both_rows, HEAD_DIM), bf16),
            pltpu.SemaphoreType.DMA((FAR_HEADS + 3 * heads,)),
        ],
        compiler_params=pltpu.CompilerParams(
            collective_id=0,
            has_side_effects=True,
        ),
    )(
        gate_input,
        value_input,
        long_filter,
        key_matrix,
        value_matrix,
        short_filter,
        query_weight,
        table,
    )


def shards(count, groups, gate_input, *others):
    rows, local_width = gate_input.shape
    by_heads = local_width % (count * groups * HEAD_DIM) == 0
    by_rows = rows >= TAPS and rows % HEAD_DIM == 0
    two_pairs = count == 4 and groups == 2
    if two_pairs and by_heads and by_rows:
        return head_shards(count, gate_input, *others)
    return general_shards(gate_input, *others)


def solution(mesh):
    in_specs = (
        P(("groups", "seq"), "chan"),
        P(("groups", "seq"), "chan"),
        P("chan", None),
        P("seq", "chan"),
        P("chan", None, None),
        P(("groups", "seq"), "chan"),
        P(("groups", "seq"), "chan"),
    )
    out_specs = P(("groups", "seq"), "chan")
    return jax.shard_map(
        functools.partial(shards, mesh.shape["seq"], mesh.shape["groups"]), mesh=mesh, in_specs=in_specs, out_specs=out_specs, check_vma=False)
```
